32 devices in a mesh: groups: 2 (over y), blk: 16 (over z, x, core), sp: 1.
Axes of the slice: x: 2, y: 2, z: 4, core: 2. Of those that a mesh axis runs over, the one named last changes fastest.
Arguments:
- out_grad: bfloat16 [8192, 1024], P(('groups', 'blk', 'sp')), parts along dimension 0, may hold values from -48 to 48
- query_act: bfloat16 [8192, 1024], P(('groups', 'blk'), 'sp'), parts along dimension 0, may hold values from -54 to 54
- key_act: bfloat16 [8192, 1024], P(('groups', 'blk'), 'sp'), parts along dimension 0, may hold values from -6 to 6
- value_act: bfloat16 [8192, 1024], P(('groups', 'blk'), 'sp'), parts along dimension 0, may hold values from -6 to 6
- out_weight: bfloat16 [1024, 1024], P('sp'), may hold values from -0.1875 to 0.1875
- query_weight: bfloat16 [1024, 1024], P(None, 'sp'), may hold values from -0.1875 to 0.1875
- key_weight: bfloat16 [1024, 1024], P(None, 'sp'), may hold values from -0.1875 to 0.1875
- value_weight: bfloat16 [1024, 1024], P(None, 'sp'), may hold values from -0.1875 to 0.1875
- neighbours: int32 [64, 8], P('groups'), parts along dimension 0, may hold values from 0 to 31, as said below
- block_counts: int32 [64], P('groups'), parts along dimension 0, may hold values from 1 to 8, as said below
Outputs:
- input_grad: bfloat16 [8192, 1024], P(('groups', 'blk', 'sp')), parts along dimension 0
The draws below stay inside these ranges and needn't reach their ends.
There are 2 independent parts, one for each index of `groups`. The reference program is written for one: setup_inputs(seed, part) draws one part's arguments, and reference() takes and returns one part's arrays. A program takes and returns all parts, laid end to end along the dimension named above; an argument that names none is the same for every part. Nothing has to cross between parts.
Inputs may be any that keep to these rules, and one draw needn't show every extreme that they name: `neighbours`: entry 0 of each row is the query block itself; the live entries of a row are distinct blocks within 8 blocks of it, counted cyclically over 32 blocks; entries at or beyond the row's count hold the block itself. `block_counts`: in every draw at least one index of blk has both of its 2 blocks (starting at a multiple of 2) with 8 live slots; other blocks may have any count from 1 to 8.
All inputs are finite; a program needn't handle non-finite values.
Results may differ from the reference program's by a relative error of at most 0.009.
Values may be sent and summed in bfloat16 or wider, within the bound.
No kernel may reach another device: no remote copies, remote signals or barrier semaphores. Data moves between devices by JAX's collectives and lax.ppermute only.
A program may use at most 128 MiB of HBM per device.

```python
import math
import jax
import jax.numpy as jnp
from jax import lax

D = 1024
HEADS = 8
HD = 128
BLOCK = 128
NBR = 8
WIN = 8
QBLK = 2
NBLK = 32
SEQ = 4096
FEAT = 1024


def pattern_pair(key):
    base_key = jax.random.fold_in(key, 17)
    key_order, key_lower, key_upper, key_hot = jax.random.split(base_key, 4)
    block_ids = jnp.arange(NBLK, dtype=jnp.int32)
    candidates = jnp.concatenate((jnp.arange(-WIN, 0), jnp.arange(1, WIN + 1))).astype(jnp.int32)
    raw_scores = jax.random.randint(key_order, (NBLK, 2 * WIN), 0, 1 << 20)
    distinct = raw_scores * (2 * WIN) + jnp.arange(2 * WIN, dtype=jnp.int32)[None, :]
    ranking = jnp.argsort(distinct, axis=1, stable=True)
    chosen = jnp.take(candidates, ranking[:, :NBR - 1])
    listed = jnp.concatenate((jnp.zeros((NBLK, 1), jnp.int32), chosen), axis=1)
    lower_draw = jax.random.randint(key_lower, (NBLK,), 0, NBR)
    upper_draw = jax.random.randint(key_upper, (NBLK,), 0, NBR)
    counts_out = 1 + jnp.minimum(lower_draw, upper_draw)
    hot_device = jax.random.randint(key_hot, (), 0, NBLK // QBLK)
    counts_out = jnp.where(block_ids // QBLK == hot_device, NBR, counts_out)
    slot_ids = jnp.arange(NBR, dtype=jnp.int32)[None, :]
    offsets = jnp.where(slot_ids < counts_out[:, None], listed, 0)
    lists_out = (block_ids[:, None] + offsets) % NBLK
    return (lists_out.astype(jnp.int32), counts_out.astype(jnp.int32))


def draw_neighbours(key, part):
    return pattern_pair(key)[0]


def draw_block_counts(key, part):
    return pattern_pair(key)[1]


def query_key_pair(key):
    base_key = jax.random.fold_in(key, 29)
    key_query, key_keys = jax.random.split(base_key)
    array_shape = (SEQ, HEADS * HD)
    keys_out = jnp.clip(jax.random.normal(key_keys, array_shape, jnp.float32), -6.0, 6.0)
    query_out = jnp.clip(jax.random.normal(key_query, array_shape, jnp.float32), -6.0, 6.0)
    return (query_out, keys_out)


def draw_query_act(key, part):
    return query_key_pair(key)[0].astype(jnp.bfloat16)


def draw_key_act(key, part):
    return query_key_pair(key)[1].astype(jnp.bfloat16)


def levels(rng, dims, shards, smallest, largest):
    gain, own = 1.0, jax.random.fold_in(rng, 6)
    for position, blocks in shards:
        steps = jnp.exp(jax.random.uniform(jax.random.fold_in(own, position), (blocks,), jnp.float32, smallest / len(shards), largest / len(shards)))
        gain = gain * jnp.repeat(steps, dims[position] // blocks).reshape([-1 if axis == position else 1 for axis in range(len(dims))])
    return gain


def centred(stream_key, shape, spread, limit, cuts=(), kind=jnp.bfloat16):
    level = levels(stream_key, shape, cuts, -0.22, 0.18) if cuts else 1.0
    result = jax.random.normal(stream_key, shape, jnp.float32) * spread * level
    return jnp.minimum(jnp.maximum(result, -limit), limit).astype(kind)


def setup_inputs(seed: int = 0, part: int = 0) -> dict:
    splits = jax.random.split(jax.random.key(seed), 11)
    part_keys = jax.random.split(jax.random.fold_in(splits[10], part), 11)
    out_grad = centred(part_keys[0], (SEQ, D), 8.0, 48.0, ((0, 16),))
    query_act = draw_query_act(jax.random.fold_in(jax.random.fold_in(splits[10], part), 71), part)
    key_act = draw_key_act(jax.random.fold_in(jax.random.fold_in(splits[10], part), 71), part)
    value_act = centred(part_keys[3], (SEQ, FEAT), 1.0, 6.0, ((0, 16),))
    out_weight = centred(splits[4], (FEAT, D), FEAT ** -0.5, 0.1875)
    query_weight = centred(splits[5], (D, FEAT), D ** -0.5, 0.1875)
    key_weight = centred(splits[6], (D, FEAT), D ** -0.5, 0.1875)
    value_weight = centred(splits[7], (D, FEAT), D ** -0.5, 0.1875)
    neighbours = draw_neighbours(jax.random.fold_in(jax.random.fold_in(splits[10], part), 71), part)
    block_counts = draw_block_counts(jax.random.fold_in(jax.random.fold_in(splits[10], part), 71), part)
    return dict(out_grad=out_grad, query_act=query_act, key_act=key_act, value_act=value_act, out_weight=out_weight, query_weight=query_weight, key_weight=key_weight, value_weight=value_weight, neighbours=neighbours, block_counts=block_counts)


def to_half(values):
    return lax.optimization_barrier(values.astype(jnp.bfloat16)).astype(jnp.float32)

def reference(out_grad, query_act, key_act, value_act, out_weight, query_weight, key_weight, value_weight, neighbours, block_counts):
    softmax_scale = 1.0 / math.sqrt(HD)
    attn_grad = jnp.dot(out_grad, out_weight.T, preferred_element_type=jnp.float32).astype(jnp.bfloat16)
    query_heads = query_act.reshape(NBLK, BLOCK, HEADS, HD)
    key_heads = key_act.reshape(NBLK, BLOCK, HEADS, HD)
    value_heads = value_act.reshape(NBLK, BLOCK, HEADS, HD)
    grad_heads = attn_grad.reshape(NBLK, BLOCK, HEADS, HD)
    slot_ids = jnp.arange(NBR, dtype=jnp.int32)

    def one_block(carry, block_id):
        key_sum, value_sum = carry
        listed = neighbours[block_id].astype(jnp.int32)
        live_slots = slot_ids < block_counts[block_id]
        query_rows = query_heads[block_id].astype(jnp.float32)
        grad_rows = grad_heads[block_id].astype(jnp.float32)
        key_rows = jnp.take(key_heads, listed, axis=0).astype(jnp.float32)
        value_rows = jnp.take(value_heads, listed, axis=0).astype(jnp.float32)
        scores = jnp.einsum('ihd,sjhd->hisj', query_rows, key_rows) * softmax_scale
        scores = jnp.where(live_slots[None, None, :, None], scores, -jnp.inf)
        row_peak = lax.optimization_barrier(jnp.max(scores, axis=(2, 3), keepdims=True))
        log_total = row_peak + jnp.log(lax.optimization_barrier(jnp.sum(jnp.exp(scores - row_peak), axis=(2, 3), keepdims=True)))
        soft_probs = jnp.exp(scores - log_total)
        probs_half = to_half(soft_probs)
        outputs = jnp.einsum('hisj,sjhd->ihd', probs_half, value_rows)
        row_delta = lax.optimization_barrier(jnp.sum(grad_rows * outputs, axis=2))
        prob_grad = jnp.einsum('ihd,sjhd->hisj', grad_rows, value_rows)
        dscore_half = to_half(soft_probs * (prob_grad - row_delta.T[:, :, None, None]))
        query_grad = (jnp.einsum('hisj,sjhd->ihd', dscore_half, key_rows) * softmax_scale).astype(jnp.bfloat16)
        key_part = jnp.einsum('hisj,ihd->sjhd', dscore_half, query_rows) * softmax_scale
        value_part = jnp.einsum('hisj,ihd->sjhd', probs_half, grad_rows)
        key_sum = key_sum.at[listed].add(key_part)
        value_sum = value_sum.at[listed].add(value_part)
        return ((key_sum, value_sum), query_grad)
    zeros_init = jnp.zeros((NBLK, BLOCK, HEADS, HD), jnp.float32)
    sums_out, query_grad = lax.scan(one_block, (zeros_init, zeros_init), jnp.arange(NBLK, dtype=jnp.int32))
    query_grad = query_grad.reshape(SEQ, FEAT)
    key_grad = sums_out[0].astype(jnp.bfloat16).reshape(SEQ, FEAT)
    value_grad = sums_out[1].astype(jnp.bfloat16).reshape(SEQ, FEAT)
    summed = jnp.dot(query_grad, query_weight.T, preferred_element_type=jnp.float32)
    summed = summed + jnp.dot(key_grad, key_weight.T, preferred_element_type=jnp.float32)
    summed = summed + jnp.dot(value_grad, value_weight.T, preferred_element_type=jnp.float32)
    return summed.astype(jnp.bfloat16)
```

```python
import functools
import math

import jax
import jax.numpy as jnp
from jax import lax
from jax.experimental import pallas as pl
from jax.experimental.pallas import tpu as pltpu
from jax.sharding import PartitionSpec as P

HD = 128
BLOCK = 128
NBR = 8
WIN = 8
CORES = 2
WIDTHS = (2, 4, 6, 8)
CONTRACT = (((1,), (1,)), ((), ()))
ANY = pl.BlockSpec(memory_space=pl.ANY)
VMEM = pl.BlockSpec(memory_space=pltpu.VMEM)
SMEM = pl.BlockSpec(memory_space=pltpu.SMEM)
LIMIT = pltpu.CompilerParams(vmem_limit_bytes=48 << 20)


def passed_along(shard, axis, by):
    size = lax.axis_size(axis)
    return lax.ppermute(shard, axis, [(i, (i + by) % size) for i in range(size)])


def rotated(chip, step, chips):
    return lax.rem(chip + step, chips)


def columns(head):
    return pl.ds(pl.multiple_of(head * HD, HD), HD)


def rows_of(block, size):
    return pl.ds(pl.multiple_of(block * size, size), size)


def pack_kernel(chips, chip_ref, *refs):
    sources, outs, sem = refs[:3], refs[3 : 3 + chips], refs[-1]
    copies = []
    for step in range(chips):
        head = rotated(chip_ref[0], step, chips)
        for place, source in enumerate(sources):
            copies.append(
                pltpu.make_async_copy(
                    source.at[:, columns(head)],
                    outs[step].at[place],
                    sem.at[step * 3 + place],
                )
            )
    for copy in copies:
        copy.start()
    for copy in copies:
        copy.wait()


def grad_kernel(chips, chip_ref, grad_ref, weight_ref, *outs):
    for step in range(chips):
        head = rotated(chip_ref[0], step, chips)
        outs[step][...] = lax.dot_general(
            grad_ref[...],
            weight_ref[rows_of(head, HD), :],
            CONTRACT,
            preferred_element_type=jnp.float32,
        ).astype(jnp.bfloat16)


def assemble_kernel(chips, tokens, chip_ref, *refs):
    pieces, (query_ref, pair_ref), sem = refs[:chips], refs[chips:-1], refs[-1]
    copies = []
    for step in range(chips):
        source = rotated(chip_ref[0], chips - step, chips)
        for place in range(3):
            target = query_ref if place == 0 else pair_ref.at[place - 1]
            copies.append(
                pltpu.make_async_copy(
                    pieces[step].at[place],
                    target.at[rows_of(source, tokens)],
                    sem.at[step * 3 + place],
                )
            )
    for copy in copies:
        copy.start()
    for copy in copies:
        copy.wait()


def attention_kernel(
    chips, tokens, scale, chip_ref, table_ref, count_ref, query_ref, own_ref, other_ref, *refs
):
    grads = refs[:chips]
    dq_ref, own_out, other_out = refs[chips : chips + 3]
    grad_buf, key_buf, value_buf, dk_buf, dv_buf, sem = refs[chips + 3 :]
    blocks = chips * tokens // BLOCK
    copies = [
        pltpu.make_async_copy(
            grads[step],
            grad_buf.at[rows_of(rotated(chip_ref[0], chips - step, chips), tokens)],
            sem.at[step],
        )
        for step in range(chips)
    ]
    half = blocks * BLOCK
    for place, buf in ((0, key_buf), (1, value_buf)):
        for side, source in ((0, own_ref), (1, other_ref)):
            copies.append(
                pltpu.make_async_copy(
                    source.at[place],
                    buf.at[pl.ds(side * half, half)],
                    sem.at[chips + 2 * place + side],
                )
            )
    for copy in copies:
        copy.start()
    dk_buf[...] = jnp.zeros_like(dk_buf)
    dv_buf[...] = jnp.zeros_like(dv_buf)
    for copy in copies:
        copy.wait()

    def attend(block, count, width):
        slots = [rows_of(table_ref[block * NBR + slot], BLOCK) for slot in range(width)]
        query = query_ref[rows_of(block, BLOCK), :]
        grad = grad_buf[rows_of(block, BLOCK), :]
        keys = jnp.concatenate([key_buf[slot, :] for slot in slots], axis=0)
        values = jnp.concatenate([value_buf[slot, :] for slot in slots], axis=0)
        scores = lax.dot_general(keys, query, CONTRACT, preferred_element_type=jnp.float32)
        live = lax.broadcasted_iota(jnp.int32, scores.shape, 0) < count * BLOCK
        scores = jnp.where(live, scores, -jnp.inf)
        peak = jnp.max(scores, axis=0, keepdims=True)
        weights = jnp.exp((scores - peak) * scale)
        probs = weights * (1.0 / jnp.sum(weights, axis=0, keepdims=True))
        half_probs = probs.astype(jnp.bfloat16)
        prob_grad = lax.dot_general(values, grad, CONTRACT, preferred_element_type=jnp.float32)
        delta = jnp.sum(half_probs.astype(jnp.float32) * prob_grad, axis=0, keepdims=True)
        dscore = (probs * (prob_grad - delta)).astype(jnp.bfloat16)
        dv = jnp.dot(half_probs, grad, preferred_element_type=jnp.float32)
        dk = jnp.dot(dscore, query, preferred_element_type=jnp.float32)
        dq = lax.dot_general(
            dscore, keys, (((0,), (0,)), ((), ())), preferred_element_type=jnp.float32
        )
        dq_ref[rows_of(block, BLOCK), :] = (dq * scale).astype(jnp.bfloat16)
        for place, slot in enumerate(slots):
            part = slice(place * BLOCK, (place + 1) * BLOCK)
            dk_buf[slot, :] += dk[part]
            dv_buf[slot, :] += dv[part]

    def one_block(block, carry):
        count = count_ref[block]
        below = 0
        for width in WIDTHS:
            pl.when((count > below) & (count <= width))(
                functools.partial(attend, block, count, width)
            )
            below = width
        return carry

    lax.fori_loop(0, blocks, one_block, 0)
    for place, buf, factor in ((0, dk_buf, scale), (1, dv_buf, 1.0)):
        own_out[place] = buf[:half] * factor
        other_out[place] = (buf[half:] * factor).astype(jnp.bfloat16)


def combine_kernel(chips, tokens, chip_ref, dq_ref, own_ref, other_ref, *outs):
    for step in range(chips):
        rows = rows_of(rotated(chip_ref[0], chips - step, chips), tokens)
        outs[step][0] = dq_ref[rows, :]
        for place in range(2):
            outs[step][place + 1] = (
                own_ref[place, rows, :] + other_ref[place, rows, :].astype(jnp.float32)
            ).astype(jnp.bfloat16)


def project_kernel(chips, chip_ref, *refs):
    pieces, weights = refs[:chips], refs[chips : chips + 3]
    out_ref, rows_buf, sem = refs[chips + 3 :]

    @pl.when(pl.program_id(0) == 0)
    def _():
        copies = []
        for step in range(chips):
            head = rotated(chip_ref[0], step, chips)
            for place in range(3):
                copies.append(
                    pltpu.make_async_copy(
                        pieces[step].at[place],
                        rows_buf.at[place, :, columns(head)],
                        sem.at[step * 3 + place],
                    )
                )
        for copy in copies:
            copy.start()
        for copy in copies:
            copy.wait()

    total = None
    for place in range(3):
        part = lax.dot_general(
            rows_buf[place],
            weights[place][...],
            CONTRACT,
            preferred_element_type=jnp.float32,
        )
        total = part if total is None else total + part
    out_ref[...] = total.astype(jnp.bfloat16)


def head_per_chip(
    out_grad, query_act, key_act, value_act, out_weight, weights, neighbours, block_counts
):
    my_index = lax.axis_index("blk")
    chips = lax.axis_size("blk") // CORES
    tokens, features = query_act.shape
    scale = 1.0 / math.sqrt(HD)
    chip = (my_index // CORES).astype(jnp.int32).reshape(1)
    core = my_index % CORES
    per_device = tokens // BLOCK
    blocks = chips * per_device
    bf16 = functools.partial(jax.ShapeDtypeStruct, dtype=jnp.bfloat16)

    def by_chips(shard, step):
        pairs = [
            (CORES * c + k, CORES * ((c + step) % chips) + k)
            for c in range(chips)
            for k in range(CORES)
        ]
        return lax.ppermute(shard, "blk", pairs)

    def across_cores(shard):
        return lax.ppermute(shard, "blk", [(i, i ^ 1) for i in range(chips * CORES)])

    packed = pl.pallas_call(
        functools.partial(pack_kernel, chips),
        out_shape=[bf16((3, tokens, HD))] * chips,
        in_specs=[SMEM] + [ANY] * 3,
        out_specs=[ANY] * chips,
        scratch_shapes=[pltpu.SemaphoreType.DMA((3 * chips,))],
    )(chip, query_act, key_act, value_act)
    packed = [packed[0]] + [by_chips(packed[step], step) for step in range(1, chips)]
    grads = pl.pallas_call(
        functools.partial(grad_kernel, chips),
        out_shape=[bf16((tokens, HD))] * chips,
        in_specs=[SMEM, VMEM, VMEM],
        out_specs=[VMEM] * chips,
        compiler_params=LIMIT,
    )(chip, out_grad, out_weight)
    grads = [grads[0]] + [by_chips(grads[step], step) for step in range(1, chips)]
    queries, pairs = pl.pallas_call(
        functools.partial(assemble_kernel, chips, tokens),
        out_shape=[bf16((chips * tokens, HD)), bf16((2, chips * tokens, HD))],
        in_specs=[SMEM] + [ANY] * chips,
        out_specs=[ANY] * 2,
        scratch_shapes=[pltpu.SemaphoreType.DMA((3 * chips,))],
    )(chip, *packed)
    other_pairs = across_cores(pairs)

    own = neighbours.reshape(chips, CORES, per_device, NBR)
    own = lax.dynamic_index_in_dim(own, core, 1, keepdims=False)
    counts = block_counts.reshape(chips, CORES, per_device)
    counts = lax.dynamic_index_in_dim(counts, core, 1, keepdims=False).reshape(-1)
    holder = own // per_device
    table = (
        jnp.where(holder % CORES == core, 0, blocks)
        + (holder // CORES) * per_device
        + own % per_device
    ).reshape(-1)

    half = chips * tokens
    dq, own_part, other_part = pl.pallas_call(
        functools.partial(attention_kernel, chips, tokens, scale),
        out_shape=[
            bf16((half, HD)),
            jax.ShapeDtypeStruct((2, half, HD), jnp.float32),
            bf16((2, half, HD)),
        ],
        in_specs=[SMEM] * 3 + [VMEM] + [ANY] * 2 + [ANY] * chips,
        out_specs=[VMEM] * 3,
        scratch_shapes=[
            pltpu.VMEM((half, HD), jnp.bfloat16),
            pltpu.VMEM((2 * half, HD), jnp.bfloat16),
            pltpu.VMEM((2 * half, HD), jnp.bfloat16),
            pltpu.VMEM((2 * half, HD), jnp.float32),
            pltpu.VMEM((2 * half, HD), jnp.float32),
            pltpu.SemaphoreType.DMA((chips + 4,)),
        ],
        compiler_params=LIMIT,
    )(chip, table, counts, queries, pairs, other_pairs, *grads)
    arrived = across_cores(other_part)
    back = pl.pallas_call(
        functools.partial(combine_kernel, chips, tokens),
        out_shape=[bf16((3, tokens, HD))] * chips,
        in_specs=[SMEM] + [VMEM] * 3,
        out_specs=[VMEM] * chips,
        compiler_params=LIMIT,
    )(chip, dq, own_part, arrived)
    back = [back[0]] + [by_chips(back[step], chips - step) for step in range(1, chips)]
    width = 256
    whole = lambda i: (0, 0)
    return pl.pallas_call(
        functools.partial(project_kernel, chips),
        out_shape=bf16((tokens, features)),
        grid=(features // width,),
        in_specs=[SMEM] + [ANY] * chips + [pl.BlockSpec((width, features), lambda i: (i, 0))] * 3,
        out_specs=pl.BlockSpec((tokens, width), lambda i: (0, i)),
        scratch_shapes=[
            pltpu.VMEM((3, tokens, features), jnp.bfloat16),
            pltpu.SemaphoreType.DMA((3 * chips,)),
        ],
        compiler_params=LIMIT,
    )(chip, *back, *weights)


def by_window(
    out_grad, query_act, key_act, value_act, out_weight, weights, neighbours, block_counts
):
    cycle_size = lax.axis_size("blk")
    my_index = lax.axis_index("blk")
    tokens, features = query_act.shape
    head_count = features // HD
    query_blocks = tokens // BLOCK
    reach_dev = (WIN + query_blocks - 1) // query_blocks
    total_blocks = query_blocks * cycle_size
    window_blocks = (2 * reach_dev + 1) * query_blocks
    scale = 1.0 / math.sqrt(HD)
    attn_grad = lax.dot_general(
        lax.all_gather(out_grad, "sp", axis=0, tiled=True),
        out_weight,
        CONTRACT,
        preferred_element_type=jnp.float32,
    ).astype(jnp.bfloat16)
    key_value = jnp.stack((key_act, value_act))
    gathered = jnp.concatenate(
        [
            key_value if offset == 0 else passed_along(key_value, "blk", -offset)
            for offset in range(-reach_dev, reach_dev + 1)
        ],
        axis=1,
    ).reshape(2, window_blocks, BLOCK, features)
    anchor = (my_index - reach_dev) * query_blocks
    own_lists = lax.dynamic_slice_in_dim(neighbours, my_index * query_blocks, query_blocks, 0)
    own_counts = lax.dynamic_slice_in_dim(block_counts, my_index * query_blocks, query_blocks, 0)
    window_index = ((own_lists - anchor) % total_blocks).reshape(-1)
    picked = jnp.concatenate(
        [
            lax.dynamic_slice_in_dim(gathered, window_index[n], 1, 1)
            for n in range(query_blocks * NBR)
        ],
        axis=1,
    ).reshape(2, query_blocks, NBR, BLOCK, head_count, HD)
    query_heads = query_act.reshape(query_blocks, BLOCK, head_count, HD)
    grad_heads = attn_grad.reshape(query_blocks, BLOCK, head_count, HD)
    einsum = functools.partial(jnp.einsum, preferred_element_type=jnp.float32)
    scores = scale * einsum("bihd,bsjhd->bhisj", query_heads, picked[0])
    live_slots = jnp.arange(NBR)[None, :] < own_counts[:, None]
    scores = jnp.where(live_slots[:, None, None, :, None], scores, -jnp.inf)
    row_peak = jnp.max(scores, axis=(3, 4), keepdims=True)
    log_total = row_peak + jnp.log(jnp.sum(jnp.exp(scores - row_peak), axis=(3, 4), keepdims=True))
    soft_probs = jnp.exp(scores - log_total)
    probs_half = soft_probs.astype(jnp.bfloat16)
    outputs = einsum("bhisj,bsjhd->bihd", probs_half, picked[1])
    row_delta = jnp.transpose(jnp.sum(grad_heads.astype(jnp.float32) * outputs, axis=3), (0, 2, 1))
    prob_grad = einsum("bihd,bsjhd->bhisj", grad_heads, picked[1])
    dscore_half = (soft_probs * (prob_grad - row_delta[:, :, :, None, None])).astype(jnp.bfloat16)
    query_grad = scale * einsum("bhisj,bsjhd->bihd", dscore_half, picked[0])
    query_grad = query_grad.astype(jnp.bfloat16).reshape(tokens, features)
    key_slots = scale * einsum("bhisj,bihd->bsjhd", dscore_half, query_heads)
    value_slots = einsum("bhisj,bihd->bsjhd", probs_half, grad_heads)
    slot_grads = jnp.stack((key_slots, value_slots)).reshape(
        2, query_blocks * NBR, BLOCK * features
    )
    selector = (jnp.arange(window_blocks)[:, None] == window_index.reshape(1, -1)).astype(
        jnp.float32
    )
    window_grads = jnp.einsum("wn,gnc->gwc", selector, slot_grads, precision=lax.Precision.HIGHEST)
    summed = 0.0
    for offset in range(-reach_dev, reach_dev + 1):
        first = (offset + reach_dev) * query_blocks
        portion = window_grads[:, first : first + query_blocks]
        summed = summed + (portion if offset == 0 else passed_along(portion, "blk", offset))
    own_grads = summed.reshape(2, tokens, features).astype(jnp.bfloat16)
    summed_rows = 0.0
    for grad, weight in zip((query_grad, own_grads[0], own_grads[1]), weights, strict=True):
        summed_rows = summed_rows + lax.dot_general(
            grad, weight, CONTRACT, preferred_element_type=jnp.float32
        )
    input_grad = lax.psum_scatter(summed_rows, "sp", scatter_dimension=0, tiled=True)
    return input_grad.astype(jnp.bfloat16)


def body(
    out_grad,
    query_act,
    key_act,
    value_act,
    out_weight,
    query_weight,
    key_weight,
    value_weight,
    neighbours,
    block_counts,
):
    heads = query_act.shape[1] // HD
    one_head = lax.axis_size("sp") == 1 and lax.axis_size("blk") == heads * CORES
    return (head_per_chip if one_head else by_window)(
        out_grad,
        query_act,
        key_act,
        value_act,
        out_weight,
        (query_weight, key_weight, value_weight),
        neighbours,
        block_counts,
    )


def solution(mesh):
    return jax.shard_map(
        body,
        mesh=mesh,
        in_specs=(
            P(("groups", "blk", "sp"), None),
            P(("groups", "blk"), "sp"),
            P(("groups", "blk"), "sp"),
            P(("groups", "blk"), "sp"),
            P("sp", None),
            P(None, "sp"),
            P(None, "sp"),
            P(None, "sp"),
            P("groups", None),
            P("groups"),
        ),
        out_specs=P(("groups", "blk", "sp"), None),
        check_vma=False,
    )
```

```python
import functools
import math

import jax
import jax.numpy as jnp
from jax import lax
from jax.experimental import pallas as pl
from jax.experimental.pallas import tpu as pltpu
from jax.sharding import PartitionSpec as P

HD = 128
BLOCK = 128
NBR = 8
WIN = 8
CORES = 2
WIDTHS = (2, 4, 6, 8)
CONTRACT = (((1,), (1,)), ((), ()))
ANY = pl.BlockSpec(memory_space=pl.ANY)
VMEM = pl.BlockSpec(memory_space=pltpu.VMEM)
SMEM = pl.BlockSpec(memory_space=pltpu.SMEM)
LIMIT = pltpu.CompilerParams(vmem_limit_bytes=48 << 20)


def passed_along(shard, axis, by):
    size = lax.axis_size(axis)
    return lax.ppermute(shard, axis, [(i, (i + by) % size) for i in range(size)])


def rotated(chip, step, chips):
    return lax.rem(chip + step, chips)


def columns(head):
    return pl.ds(pl.multiple_of(head * HD, HD), HD)


def rows_of(block, size):
    return pl.ds(pl.multiple_of(block * size, size), size)


def pack_kernel(chips, chip_ref, *refs):
    sources, outs = refs[:3], refs[3:]
    for step in range(chips):
        head = rotated(chip_ref[0], step, chips)
        for place, source in enumerate(sources):
            outs[step][place] = source[:, columns(head)]


def grad_kernel(chips, chip_ref, grad_ref, weight_ref, *outs):
    for step in range(chips):
        head = rotated(chip_ref[0], step, chips)
        outs[step][...] = lax.dot_general(
            grad_ref[...],
            weight_ref[rows_of(head, HD), :],
            CONTRACT,
            preferred_element_type=jnp.float32,
        ).astype(jnp.bfloat16)


def assemble_kernel(chips, tokens, chip_ref, *refs):
    pieces, (query_ref, pair_ref) = refs[:chips], refs[chips:]
    for step in range(chips):
        rows = rows_of(rotated(chip_ref[0], chips - step, chips), tokens)
        query_ref[rows, :] = pieces[step][0]
        for place in range(2):
            pair_ref[place, rows, :] = pieces[step][place + 1]


def attention_kernel(
    chips, tokens, scale, chip_ref, table_ref, count_ref, query_ref, own_ref, other_ref, *refs
):
    grads = refs[:chips]
    dq_ref, own_out, other_out = refs[chips : chips + 3]
    grad_buf, key_buf, value_buf, dk_buf, dv_buf, sem = refs[chips + 3 :]
    blocks = chips * tokens // BLOCK
    copies = [
        pltpu.make_async_copy(
            grads[step],
            grad_buf.at[rows_of(rotated(chip_ref[0], chips - step, chips), tokens)],
            sem.at[step],
        )
        for step in range(chips)
    ]
    half = blocks * BLOCK
    for place, buf in ((0, key_buf), (1, value_buf)):
        for side, source in ((0, own_ref), (1, other_ref)):
            copies.append(
                pltpu.make_async_copy(
                    source.at[place],
                    buf.at[pl.ds(side * half, half)],
                    sem.at[chips + 2 * place + side],
                )
            )
    for copy in copies:
        copy.start()
    dk_buf[...] = jnp.zeros_like(dk_buf)
    dv_buf[...] = jnp.zeros_like(dv_buf)
    for copy in copies:
        copy.wait()

    def attend(block, count, width):
        slots = [rows_of(table_ref[block * NBR + slot], BLOCK) for slot in range(width)]
        query = query_ref[rows_of(block, BLOCK), :]
        grad = grad_buf[rows_of(block, BLOCK), :]
        keys = jnp.concatenate([key_buf[slot, :] for slot in slots], axis=0)
        values = jnp.concatenate([value_buf[slot, :] for slot in slots], axis=0)
        scores = lax.dot_general(keys, query, CONTRACT, preferred_element_type=jnp.float32)
        live = lax.broadcasted_iota(jnp.int32, scores.shape, 0) < count * BLOCK
        scores = jnp.where(live, scores, -jnp.inf)
        peak = jnp.max(scores, axis=0, keepdims=True)
        weights = jnp.exp((scores - peak) * scale)
        probs = weights * (1.0 / jnp.sum(weights, axis=0, keepdims=True))
        half_probs = probs.astype(jnp.bfloat16)
        prob_grad = lax.dot_general(values, grad, CONTRACT, preferred_element_type=jnp.float32)
        delta = jnp.sum(half_probs.astype(jnp.float32) * prob_grad, axis=0, keepdims=True)
        dscore = (probs * (prob_grad - delta)).astype(jnp.bfloat16)
        dv = jnp.dot(half_probs, grad, preferred_element_type=jnp.float32)
        dk = jnp.dot(dscore, query, preferred_element_type=jnp.float32)
        dq = lax.dot_general(
            dscore, keys, (((0,), (0,)), ((), ())), preferred_element_type=jnp.float32
        )
        dq_ref[rows_of(block, BLOCK), :] = (dq * scale).astype(jnp.bfloat16)
        for place, slot in enumerate(slots):
            part = slice(place * BLOCK, (place + 1) * BLOCK)
            dk_buf[slot, :] += dk[part]
            dv_buf[slot, :] += dv[part]

    def one_block(block, carry):
        count = count_ref[block]
        below = 0
        for width in WIDTHS:
            pl.when((count > below) & (count <= width))(
                functools.partial(attend, block, count, width)
            )
            below = width
        return carry

    lax.fori_loop(0, blocks, one_block, 0)
    for place, buf, factor in ((0, dk_buf, scale), (1, dv_buf, 1.0)):
        own_out[place] = buf[:half] * factor
        other_out[place] = (buf[half:] * factor).astype(jnp.bfloat16)


def combine_kernel(chips, tokens, chip_ref, dq_ref, own_ref, other_ref, *outs):
    for step in range(chips):
        rows = rows_of(rotated(chip_ref[0], chips - step, chips), tokens)
        outs[step][0] = dq_ref[rows, :]
        for place in range(2):
            outs[step][place + 1] = (
                own_ref[place, rows, :] + other_ref[place, rows, :].astype(jnp.float32)
            ).astype(jnp.bfloat16)


def project_kernel(chips, chip_ref, *refs):
    pieces, weights = refs[:chips], refs[chips : chips + 3]
    out_ref, rows_buf, sem = refs[chips + 3 :]

    @pl.when(pl.program_id(0) == 0)
    def _():
        copies = []
        for step in range(chips):
            head = rotated(chip_ref[0], step, chips)
            for place in range(3):
                copies.append(
                    pltpu.make_async_copy(
                        pieces[step].at[place],
                        rows_buf.at[place, :, columns(head)],
                        sem.at[step * 3 + place],
                    )
                )
        for copy in copies:
            copy.start()
        for copy in copies:
            copy.wait()

    total = None
    for place in range(3):
        part = lax.dot_general(
            rows_buf[place],
            weights[place][...],
            CONTRACT,
            preferred_element_type=jnp.float32,
        )
        total = part if total is None else total + part
    out_ref[...] = total.astype(jnp.bfloat16)


def head_per_chip(
    out_grad, query_act, key_act, value_act, out_weight, weights, neighbours, block_counts
):
    my_index = lax.axis_index("blk")
    chips = lax.axis_size("blk") // CORES
    tokens, features = query_act.shape
    scale = 1.0 / math.sqrt(HD)
    chip = (my_index // CORES).astype(jnp.int32).reshape(1)
    core = my_index % CORES
    per_device = tokens // BLOCK
    blocks = chips * per_device
    bf16 = functools.partial(jax.ShapeDtypeStruct, dtype=jnp.bfloat16)

    def by_chips(shard, step):
        pairs = [
            (CORES * c + k, CORES * ((c + step) % chips) + k)
            for c in range(chips)
            for k in range(CORES)
        ]
        return lax.ppermute(shard, "blk", pairs)

    def across_cores(shard):
        return lax.ppermute(shard, "blk", [(i, i ^ 1) for i in range(chips * CORES)])

    packed = pl.pallas_call(
        functools.partial(pack_kernel, chips),
        out_shape=[bf16((3, tokens, HD))] * chips,
        in_specs=[SMEM] + [VMEM] * 3,
        out_specs=[VMEM] * chips,
        compiler_params=LIMIT,
    )(chip, query_act, key_act, value_act)
    packed = [packed[0]] + [by_chips(packed[step], step) for step in range(1, chips)]
    grads = pl.pallas_call(
        functools.partial(grad_kernel, chips),
        out_shape=[bf16((tokens, HD))] * chips,
        in_specs=[SMEM, VMEM, VMEM],
        out_specs=[VMEM] * chips,
        compiler_params=LIMIT,
    )(chip, out_grad, out_weight)
    packed, _ = lax.optimization_barrier((packed, grads))
    grads = [grads[0]] + [by_chips(grads[step], step) for step in range(1, chips)]
    queries, pairs = pl.pallas_call(
        functools.partial(assemble_kernel, chips, tokens),
        out_shape=[bf16((chips * tokens, HD)), bf16((2, chips * tokens, HD))],
        in_specs=[SMEM] + [VMEM] * chips,
        out_specs=[VMEM] * 2,
        compiler_params=LIMIT,
    )(chip, *packed)
    other_pairs = across_cores(pairs)

    own = neighbours.reshape(chips, CORES, per_device, NBR)
    own = lax.dynamic_index_in_dim(own, core, 1, keepdims=False)
    counts = block_counts.reshape(chips, CORES, per_device)
    counts = lax.dynamic_index_in_dim(counts, core, 1, keepdims=False).reshape(-1)
    holder = own // per_device
    table = (
        jnp.where(holder % CORES == core, 0, blocks)
        + (holder // CORES) * per_device
        + own % per_device
    ).reshape(-1)

    half = chips * tokens
    dq, own_part, other_part = pl.pallas_call(
        functools.partial(attention_kernel, chips, tokens, scale),
        out_shape=[
            bf16((half, HD)),
            jax.ShapeDtypeStruct((2, half, HD), jnp.float32),
            bf16((2, half, HD)),
        ],
        in_specs=[SMEM] * 3 + [VMEM] + [ANY] * 2 + [ANY] * chips,
        out_specs=[VMEM] * 3,
        scratch_shapes=[
            pltpu.VMEM((half, HD), jnp.bfloat16),
            pltpu.VMEM((2 * half, HD), jnp.bfloat16),
            pltpu.VMEM((2 * half, HD), jnp.bfloat16),
            pltpu.VMEM((2 * half, HD), jnp.float32),
            pltpu.VMEM((2 * half, HD), jnp.float32),
            pltpu.SemaphoreType.DMA((chips + 4,)),
        ],
        compiler_params=LIMIT,
    )(chip, table, counts, queries, pairs, other_pairs, *grads)
    arrived = across_cores(other_part)
    back = pl.pallas_call(
        functools.partial(combine_kernel, chips, tokens),
        out_shape=[bf16((3, tokens, HD))] * chips,
        in_specs=[SMEM] + [VMEM] * 3,
        out_specs=[VMEM] * chips,
        compiler_params=LIMIT,
    )(chip, dq, own_part, arrived)
    back = [back[0]] + [by_chips(back[step], chips - step) for step in range(1, chips)]
    width = 256
    whole = lambda i: (0, 0)
    return pl.pallas_call(
        functools.partial(project_kernel, chips),
        out_shape=bf16((tokens, features)),
        grid=(features // width,),
        in_specs=[SMEM] + [ANY] * chips + [pl.BlockSpec((width, features), lambda i: (i, 0))] * 3,
        out_specs=pl.BlockSpec((tokens, width), lambda i: (0, i)),
        scratch_shapes=[
            pltpu.VMEM((3, tokens, features), jnp.bfloat16),
            pltpu.SemaphoreType.DMA((3 * chips,)),
        ],
        compiler_params=LIMIT,
    )(chip, *back, *weights)


def by_window(
    out_grad, query_act, key_act, value_act, out_weight, weights, neighbours, block_counts
):
    cycle_size = lax.axis_size("blk")
    my_index = lax.axis_index("blk")
    tokens, features = query_act.shape
    head_count = features // HD
    query_blocks = tokens // BLOCK
    reach_dev = (WIN + query_blocks - 1) // query_blocks
    total_blocks = query_blocks * cycle_size
    window_blocks = (2 * reach_dev + 1) * query_blocks
    scale = 1.0 / math.sqrt(HD)
    attn_grad = lax.dot_general(
        lax.all_gather(out_grad, "sp", axis=0, tiled=True),
        out_weight,
        CONTRACT,
        preferred_element_type=jnp.float32,
    ).astype(jnp.bfloat16)
    key_value = jnp.stack((key_act, value_act))
    gathered = jnp.concatenate(
        [
            key_value if offset == 0 else passed_along(key_value, "blk", -offset)
            for offset in range(-reach_dev, reach_dev + 1)
        ],
        axis=1,
    ).reshape(2, window_blocks, BLOCK, features)
    anchor = (my_index - reach_dev) * query_blocks
    own_lists = lax.dynamic_slice_in_dim(neighbours, my_index * query_blocks, query_blocks, 0)
    own_counts = lax.dynamic_slice_in_dim(block_counts, my_index * query_blocks, query_blocks, 0)
    window_index = ((own_lists - anchor) % total_blocks).reshape(-1)
    picked = jnp.concatenate(
        [
            lax.dynamic_slice_in_dim(gathered, window_index[n], 1, 1)
            for n in range(query_blocks * NBR)
        ],
        axis=1,
    ).reshape(2, query_blocks, NBR, BLOCK, head_count, HD)
    query_heads = query_act.reshape(query_blocks, BLOCK, head_count, HD)
    grad_heads = attn_grad.reshape(query_blocks, BLOCK, head_count, HD)
    einsum = functools.partial(jnp.einsum, preferred_element_type=jnp.float32)
    scores = scale * einsum("bihd,bsjhd->bhisj", query_heads, picked[0])
    live_slots = jnp.arange(NBR)[None, :] < own_counts[:, None]
    scores = jnp.where(live_slots[:, None, None, :, None], scores, -jnp.inf)
    row_peak = jnp.max(scores, axis=(3, 4), keepdims=True)
    log_total = row_peak + jnp.log(jnp.sum(jnp.exp(scores - row_peak), axis=(3, 4), keepdims=True))
    soft_probs = jnp.exp(scores - log_total)
    probs_half = soft_probs.astype(jnp.bfloat16)
    outputs = einsum("bhisj,bsjhd->bihd", probs_half, picked[1])
    row_delta = jnp.transpose(jnp.sum(grad_heads.astype(jnp.float32) * outputs, axis=3), (0, 2, 1))
    prob_grad = einsum("bihd,bsjhd->bhisj", grad_heads, picked[1])
    dscore_half = (soft_probs * (prob_grad - row_delta[:, :, :, None, None])).astype(jnp.bfloat16)
    query_grad = scale * einsum("bhisj,bsjhd->bihd", dscore_half, picked[0])
    query_grad = query_grad.astype(jnp.bfloat16).reshape(tokens, features)
    key_slots = scale * einsum("bhisj,bihd->bsjhd", dscore_half, query_heads)
    value_slots = einsum("bhisj,bihd->bsjhd", probs_half, grad_heads)
    slot_grads = jnp.stack((key_slots, value_slots)).reshape(
        2, query_blocks * NBR, BLOCK * features
    )
    selector = (jnp.arange(window_blocks)[:, None] == window_index.reshape(1, -1)).astype(
        jnp.float32
    )
    window_grads = jnp.einsum("wn,gnc->gwc", selector, slot_grads, precision=lax.Precision.HIGHEST)
    summed = 0.0
    for offset in range(-reach_dev, reach_dev + 1):
        first = (offset + reach_dev) * query_blocks
        portion = window_grads[:, first : first + query_blocks]
        summed = summed + (portion if offset == 0 else passed_along(portion, "blk", offset))
    own_grads = summed.reshape(2, tokens, features).astype(jnp.bfloat16)
    summed_rows = 0.0
    for grad, weight in zip((query_grad, own_grads[0], own_grads[1]), weights, strict=True):
        summed_rows = summed_rows + lax.dot_general(
            grad, weight, CONTRACT, preferred_element_type=jnp.float32
        )
    input_grad = lax.psum_scatter(summed_rows, "sp", scatter_dimension=0, tiled=True)
    return input_grad.astype(jnp.bfloat16)


def body(
    out_grad,
    query_act,
    key_act,
    value_act,
    out_weight,
    query_weight,
    key_weight,
    value_weight,
    neighbours,
    block_counts,
):
    heads = query_act.shape[1] // HD
    one_head = lax.axis_size("sp") == 1 and lax.axis_size("blk") == heads * CORES
    return (head_per_chip if one_head else by_window)(
        out_grad,
        query_act,
        key_act,
        value_act,
        out_weight,
        (query_weight, key_weight, value_weight),
        neighbours,
        block_counts,
    )


def solution(mesh):
    return jax.shard_map(
        body,
        mesh=mesh,
        in_specs=(
            P(("groups", "blk", "sp"), None),
            P(("groups", "blk"), "sp"),
            P(("groups", "blk"), "sp"),
            P(("groups", "blk"), "sp"),
            P("sp", None),
            P(None, "sp"),
            P(None, "sp"),
            P(None, "sp"),
            P("groups", None),
            P("groups"),
        ),
        out_specs=P(("groups", "blk", "sp"), None),
        check_vma=False,
    )
```

```python
import functools
import math

import jax
import jax.numpy as jnp
from jax import lax
from jax.experimental import pallas as pl
from jax.experimental.pallas import tpu as pltpu
from jax.sharding import PartitionSpec as P

HD = 128
BLOCK = 128
NBR = 8
WIN = 8
CORES = 2
WIDTHS = (2, 4, 6, 8)
CONTRACT = (((1,), (1,)), ((), ()))
ANY = pl.BlockSpec(memory_space=pltpu.HBM)
VMEM = pl.BlockSpec(memory_space=pltpu.VMEM)
SMEM = pl.BlockSpec(memory_space=pltpu.SMEM)
LIMIT = pltpu.CompilerParams(vmem_limit_bytes=48 << 20)


def passed_along(shard, axis, by):
    size = lax.axis_size(axis)
    return lax.ppermute(shard, axis, [(i, (i + by) % size) for i in range(size)])


def rotated(chip, step, chips):
    return lax.rem(chip + step, chips)


def columns(head):
    return pl.ds(pl.multiple_of(head * HD, HD), HD)


def rows_of(block, size):
    return pl.ds(pl.multiple_of(block * size, size), size)


def pack_kernel(chips, chip_ref, *refs):
    sources, outs, sem = refs[:2], refs[2:-1], refs[-1]
    copies = [
        pltpu.make_async_copy(
            source.at[:, columns(rotated(chip_ref[0], step, chips))],
            outs[step].at[place],
            sem.at[step * 2 + place],
        )
        for step in range(chips)
        for place, source in enumerate(sources)
    ]
    for copy in copies:
        copy.start()
    for copy in copies:
        copy.wait()


def grad_kernel(chips, chip_ref, grad_ref, weight_ref, value_ref, *outs):
    for step in range(chips):
        head = rotated(chip_ref[0], step, chips)
        outs[step][0] = value_ref[:, columns(head)]
        outs[step][1] = lax.dot_general(
            grad_ref[...],
            weight_ref[rows_of(head, HD), :],
            CONTRACT,
            preferred_element_type=jnp.float32,
        ).astype(jnp.bfloat16)


def in_order(chips, tokens, chip_ref, pieces, place, target, first=0):
    for step in range(chips):
        source = rotated(chip_ref[0], chips - step, chips)
        rows = pl.ds(pl.multiple_of(first + source * tokens, tokens), tokens)
        target[rows, :] = pieces[step][place]


def assemble_kernel(chips, tokens, place, chip_ref, *refs):
    in_order(chips, tokens, chip_ref, refs[:chips], place, refs[chips])


def by_width(count_ref, blocks, work):
    def one_block(block, carry):
        count = count_ref[block]
        below = 0
        for width in WIDTHS:
            pl.when((count > below) & (count <= width))(
                functools.partial(work, block, count, width)
            )
            below = width
        return carry

    lax.fori_loop(0, blocks, one_block, 0)


def slots_of(table_ref, block, width):
    return [rows_of(table_ref[block * NBR + slot], BLOCK) for slot in range(width)]


def prob_rows(block, width):
    return pl.ds(pl.multiple_of(block * NBR * BLOCK, NBR * BLOCK), width * BLOCK)


def prob_kernel(chips, tokens, scale, chip_ref, table_ref, count_ref, *refs):
    pieces, (other_ref, prob_ref, query_buf, key_buf) = refs[:chips], refs[chips:]
    half = chips * tokens
    in_order(chips, tokens, chip_ref, pieces, 0, query_buf)
    in_order(chips, tokens, chip_ref, pieces, 1, key_buf)
    key_buf[half:] = other_ref[...]

    def work(block, count, width):
        query = query_buf[rows_of(block, BLOCK), :]
        keys = jnp.concatenate(
            [key_buf[slot, :] for slot in slots_of(table_ref, block, width)], axis=0
        )
        scores = lax.dot_general(keys, query, CONTRACT, preferred_element_type=jnp.float32)
        live = lax.broadcasted_iota(jnp.int32, scores.shape, 0) < count * BLOCK
        scores = jnp.where(live, scores, -jnp.inf)
        peak = jnp.max(scores, axis=0, keepdims=True)
        weights = jnp.exp((scores - peak) * scale)
        probs = weights * (1.0 / jnp.sum(weights, axis=0, keepdims=True))
        prob_ref[prob_rows(block, width), :] = probs.astype(jnp.bfloat16)

    by_width(count_ref, half // BLOCK, work)


def value_kernel(chips, tokens, chip_ref, table_ref, count_ref, prob_ref, *refs):
    pieces, (own_out, other_out, grad_buf, total) = refs[:chips], refs[chips:]
    half = chips * tokens
    in_order(chips, tokens, chip_ref, pieces, 1, grad_buf)
    total[...] = jnp.zeros_like(total)

    def work(block, count, width):
        grad = grad_buf[rows_of(block, BLOCK), :]
        part = jnp.dot(
            prob_ref[prob_rows(block, width), :], grad, preferred_element_type=jnp.float32
        )
        for place, slot in enumerate(slots_of(table_ref, block, width)):
            total[slot, :] += part[place * BLOCK : (place + 1) * BLOCK]

    by_width(count_ref, half // BLOCK, work)
    own_out[...] = total[:half]
    other_out[...] = total[half:].astype(jnp.bfloat16)


def score_kernel(chips, tokens, scale, chip_ref, table_ref, count_ref, prob_ref, *refs):
    firsts, seconds = refs[:chips], refs[chips : 2 * chips]
    other_key, other_value, dq_ref, own_out, other_out = refs[2 * chips : 2 * chips + 5]
    query_buf, grad_buf, key_buf, value_buf, total = refs[2 * chips + 5 :]
    half = chips * tokens
    in_order(chips, tokens, chip_ref, firsts, 0, query_buf)
    in_order(chips, tokens, chip_ref, firsts, 1, key_buf)
    in_order(chips, tokens, chip_ref, seconds, 0, value_buf)
    in_order(chips, tokens, chip_ref, seconds, 1, grad_buf)
    key_buf[half:] = other_key[...]
    value_buf[half:] = other_value[...]
    total[...] = jnp.zeros_like(total)

    def work(block, count, width):
        slots = slots_of(table_ref, block, width)
        rows = rows_of(block, BLOCK)
        keys = jnp.concatenate([key_buf[slot, :] for slot in slots], axis=0)
        values = jnp.concatenate([value_buf[slot, :] for slot in slots], axis=0)
        probs = prob_ref[prob_rows(block, width), :].astype(jnp.float32)
        prob_grad = lax.dot_general(
            values, grad_buf[rows, :], CONTRACT, preferred_element_type=jnp.float32
        )
        delta = jnp.sum(probs * prob_grad, axis=0, keepdims=True)
        dscore = (probs * (prob_grad - delta)).astype(jnp.bfloat16)
        dk = jnp.dot(dscore, query_buf[rows, :], preferred_element_type=jnp.float32)
        dq = lax.dot_general(
            dscore, keys, (((0,), (0,)), ((), ())), preferred_element_type=jnp.float32
        )
        dq_ref[rows, :] = (dq * scale).astype(jnp.bfloat16)
        for place, slot in enumerate(slots):
            total[slot, :] += dk[place * BLOCK : (place + 1) * BLOCK]

    by_width(count_ref, half // BLOCK, work)
    own_out[...] = total[:half] * scale
    other_out[...] = (total[half:] * scale).astype(jnp.bfloat16)


def combine_kernel(chips, tokens, chip_ref, own_ref, other_ref, *refs):
    done, outs = refs[: len(refs) - chips], refs[len(refs) - chips :]
    for step in range(chips):
        rows = rows_of(rotated(chip_ref[0], chips - step, chips), tokens)
        outs[step][0] = (own_ref[rows, :] + other_ref[rows, :].astype(jnp.float32)).astype(
            jnp.bfloat16
        )
        for place, source in enumerate(done):
            outs[step][place + 1] = source[rows, :]


def project_kernel(chips, places, chip_ref, *refs):
    pieces, weights = refs[:chips], refs[chips : chips + places]
    before, (out_ref, *rows_bufs) = refs[chips + places : -places - 1], refs[-places - 1 :]
    total = before[0][...] if before else None
    for place in range(places):
        for step in range(chips):
            head = rotated(chip_ref[0], step, chips)
            rows_bufs[place][:, columns(head)] = pieces[step][place]
        part = lax.dot_general(
            rows_bufs[place][...], weights[place][...], CONTRACT, preferred_element_type=jnp.float32
        )
        total = part if total is None else total + part
    out_ref[...] = total.astype(out_ref.dtype)


def head_per_chip(
    out_grad, query_act, key_act, value_act, out_weight, weights, neighbours, block_counts
):
    my_index = lax.axis_index("blk")
    chips = lax.axis_size("blk") // CORES
    tokens, features = query_act.shape
    scale = 1.0 / math.sqrt(HD)
    chip = (my_index // CORES).astype(jnp.int32).reshape(1)
    core = my_index % CORES
    per_device = tokens // BLOCK
    blocks = chips * per_device
    half = chips * tokens
    bf16 = functools.partial(jax.ShapeDtypeStruct, dtype=jnp.bfloat16)
    f32 = functools.partial(jax.ShapeDtypeStruct, dtype=jnp.float32)
    buf16 = functools.partial(pltpu.VMEM, dtype=jnp.bfloat16)
    buf32 = functools.partial(pltpu.VMEM, dtype=jnp.float32)

    def call(kernel, outs, scratch, scalars, *arrays, spec=VMEM):
        return pl.pallas_call(
            kernel,
            out_shape=outs,
            in_specs=[SMEM] * len(scalars) + [spec] * len(arrays),
            out_specs=jax.tree.map(lambda _: VMEM, outs),
            scratch_shapes=scratch,
            compiler_params=LIMIT,
        )(*scalars, *arrays)

    def by_chips(shard, step):
        pairs = [
            (CORES * c + k, CORES * ((c + step) % chips) + k)
            for c in range(chips)
            for k in range(CORES)
        ]
        return lax.ppermute(shard, "blk", pairs)

    def out_to(shards):
        return [shards[0]] + [by_chips(shards[step], step) for step in range(1, chips)]

    def back_to(shards):
        return [shards[0]] + [by_chips(shards[step], chips - step) for step in range(1, chips)]

    def across_cores(shard):
        return lax.ppermute(shard, "blk", [(i, i ^ 1) for i in range(chips * CORES)])

    own = neighbours.reshape(chips, CORES, per_device, NBR)
    own = lax.dynamic_index_in_dim(own, core, 1, keepdims=False)
    counts = block_counts.reshape(chips, CORES, per_device)
    counts = lax.dynamic_index_in_dim(counts, core, 1, keepdims=False).reshape(-1)
    holder = own // per_device
    table = (
        jnp.where(holder % CORES == core, 0, blocks)
        + (holder // CORES) * per_device
        + own % per_device
    ).reshape(-1)
    lists = (chip, table, counts)
    piece = [bf16((2, tokens, HD))] * chips
    partial_outs = [f32((half, HD)), bf16((half, HD))]
    args = functools.partial

    packed = call(
        args(pack_kernel, chips), piece, [pltpu.SemaphoreType.DMA((2 * chips,))],
        (chip,), query_act, key_act, spec=ANY,
    )
    firsts = out_to(packed)
    packed = call(
        args(grad_kernel, chips), piece, [], (chip,), out_grad, out_weight, value_act
    )
    firsts, _ = lax.optimization_barrier((firsts, packed))
    seconds = out_to(packed)
    keys = call(args(assemble_kernel, chips, tokens, 1), bf16((half, HD)), [], (chip,), *firsts)
    other_keys = across_cores(keys)
    probs = call(
        args(prob_kernel, chips, tokens, scale),
        bf16((blocks * NBR * BLOCK, HD)),
        [buf16((half, HD)), buf16((2 * half, HD))],
        lists, *firsts, other_keys,
    )
    seconds, probs = lax.optimization_barrier((seconds, probs))
    values = call(args(assemble_kernel, chips, tokens, 0), bf16((half, HD)), [], (chip,), *seconds)
    other_values = across_cores(values)
    own_dv, sent_dv = call(
        args(value_kernel, chips, tokens), partial_outs,
        [buf16((half, HD)), buf32((2 * half, HD))],
        lists, probs, *seconds,
    )
    came_dv = across_cores(sent_dv)
    dq, own_dk, sent_dk = call(
        args(score_kernel, chips, tokens, scale), [bf16((half, HD))] + partial_outs,
        [buf16((half, HD))] * 2 + [buf16((2 * half, HD))] * 2 + [buf32((2 * half, HD))],
        lists, probs, *firsts, *seconds, other_keys, other_values,
    )
    came_dk = across_cores(sent_dk)
    first_back = back_to(
        call(args(combine_kernel, chips, tokens), piece, [], (chip,), own_dv, came_dv, dq)
    )
    last_back = back_to(
        call(
            args(combine_kernel, chips, tokens), [bf16((1, tokens, HD))] * chips, [],
            (chip,), own_dk, came_dk,
        )
    )
    query_weight, key_weight, value_weight = weights
    rows_buf = buf16((tokens, features))
    most = call(
        args(project_kernel, chips, 2), f32((tokens, features)), [rows_buf] * 2,
        (chip,), *first_back, value_weight, query_weight,
    )
    last_back, most = lax.optimization_barrier((last_back, most))
    return call(
        args(project_kernel, chips, 1), bf16((tokens, features)), [rows_buf],
        (chip,), *last_back, key_weight, most,
    )


def by_window(
    out_grad, query_act, key_act, value_act, out_weight, weights, neighbours, block_counts
):
    cycle_size = lax.axis_size("blk")
    my_index = lax.axis_index("blk")
    tokens, features = query_act.shape
    head_count = features // HD
    query_blocks = tokens // BLOCK
    reach_dev = (WIN + query_blocks - 1) // query_blocks
    total_blocks = query_blocks * cycle_size
    window_blocks = (2 * reach_dev + 1) * query_blocks
    scale = 1.0 / math.sqrt(HD)
    attn_grad = lax.dot_general(
        lax.all_gather(out_grad, "sp", axis=0, tiled=True),
        out_weight,
        CONTRACT,
        preferred_element_type=jnp.float32,
    ).astype(jnp.bfloat16)
    key_value = jnp.stack((key_act, value_act))
    gathered = jnp.concatenate(
        [
            key_value if offset == 0 else passed_along(key_value, "blk", -offset)
            for offset in range(-reach_dev, reach_dev + 1)
        ],
        axis=1,
    ).reshape(2, window_blocks, BLOCK, features)
    anchor = (my_index - reach_dev) * query_blocks
    own_lists = lax.dynamic_slice_in_dim(neighbours, my_index * query_blocks, query_blocks, 0)
    own_counts = lax.dynamic_slice_in_dim(block_counts, my_index * query_blocks, query_blocks, 0)
    window_index = ((own_lists - anchor) % total_blocks).reshape(-1)
    picked = jnp.concatenate(
        [
            lax.dynamic_slice_in_dim(gathered, window_index[n], 1, 1)
            for n in range(query_blocks * NBR)
        ],
        axis=1,
    ).reshape(2, query_blocks, NBR, BLOCK, head_count, HD)
    query_heads = query_act.reshape(query_blocks, BLOCK, head_count, HD)
    grad_heads = attn_grad.reshape(query_blocks, BLOCK, head_count, HD)
    einsum = functools.partial(jnp.einsum, preferred_element_type=jnp.float32)
    scores = scale * einsum("bihd,bsjhd->bhisj", query_heads, picked[0])
    live_slots = jnp.arange(NBR)[None, :] < own_counts[:, None]
    scores = jnp.where(live_slots[:, None, None, :, None], scores, -jnp.inf)
    row_peak = jnp.max(scores, axis=(3, 4), keepdims=True)
    log_total = row_peak + jnp.log(jnp.sum(jnp.exp(scores - row_peak), axis=(3, 4), keepdims=True))
    soft_probs = jnp.exp(scores - log_total)
    probs_half = soft_probs.astype(jnp.bfloat16)
    outputs = einsum("bhisj,bsjhd->bihd", probs_half, picked[1])
    row_delta = jnp.transpose(jnp.sum(grad_heads.astype(jnp.float32) * outputs, axis=3), (0, 2, 1))
    prob_grad = einsum("bihd,bsjhd->bhisj", grad_heads, picked[1])
    dscore_half = (soft_probs * (prob_grad - row_delta[:, :, :, None, None])).astype(jnp.bfloat16)
    query_grad = scale * einsum("bhisj,bsjhd->bihd", dscore_half, picked[0])
    query_grad = query_grad.astype(jnp.bfloat16).reshape(tokens, features)
    key_slots = scale * einsum("bhisj,bihd->bsjhd", dscore_half, query_heads)
    value_slots = einsum("bhisj,bihd->bsjhd", probs_half, grad_heads)
    slot_grads = jnp.stack((key_slots, value_slots)).reshape(
        2, query_blocks * NBR, BLOCK * features
    )
    selector = (jnp.arange(window_blocks)[:, None] == window_index.reshape(1, -1)).astype(
        jnp.float32
    )
    window_grads = jnp.einsum("wn,gnc->gwc", selector, slot_grads, precision=lax.Precision.HIGHEST)
    summed = 0.0
    for offset in range(-reach_dev, reach_dev + 1):
        first = (offset + reach_dev) * query_blocks
        portion = window_grads[:, first : first + query_blocks]
        summed = summed + (portion if offset == 0 else passed_along(portion, "blk", offset))
    own_grads = summed.reshape(2, tokens, features).astype(jnp.bfloat16)
    summed_rows = 0.0
    for grad, weight in zip((query_grad, own_grads[0], own_grads[1]), weights, strict=True):
        summed_rows = summed_rows + lax.dot_general(
            grad, weight, CONTRACT, preferred_element_type=jnp.float32
        )
    input_grad = lax.psum_scatter(summed_rows, "sp", scatter_dimension=0, tiled=True)
    return input_grad.astype(jnp.bfloat16)


def body(
    out_grad,
    query_act,
    key_act,
    value_act,
    out_weight,
    query_weight,
    key_weight,
    value_weight,
    neighbours,
    block_counts,
):
    heads = query_act.shape[1] // HD
    one_head = lax.axis_size("sp") == 1 and lax.axis_size("blk") == heads * CORES
    return (head_per_chip if one_head else by_window)(
        out_grad,
        query_act,
        key_act,
        value_act,
        out_weight,
        (query_weight, key_weight, value_weight),
        neighbours,
        block_counts,
    )


def solution(mesh):
    return jax.shard_map(
        body,
        mesh=mesh,
        in_specs=(
            P(("groups", "blk", "sp"), None),
            P(("groups", "blk"), "sp"),
            P(("groups", "blk"), "sp"),
            P(("groups", "blk"), "sp"),
            P("sp", None),
            P(None, "sp"),
            P(None, "sp"),
            P(None, "sp"),
            P("groups", None),
            P("groups"),
        ),
        out_specs=P(("groups", "blk", "sp"), None),
        check_vma=False,
    )
```

```python
import functools
import math

import jax
import jax.numpy as jnp
from jax import lax
from jax.experimental import pallas as pl
from jax.experimental.pallas import tpu as pltpu
from jax.sharding import PartitionSpec as P

HD = 128
BLOCK = 128
NBR = 8
WIN = 8
CORES = 2
WIDTHS = (2, 4, 6, 8)
CONTRACT = (((1,), (1,)), ((), ()))
ANY = pl.BlockSpec(memory_space=pl.ANY)
VMEM = pl.BlockSpec(memory_space=pltpu.VMEM)
SMEM = pl.BlockSpec(memory_space=pltpu.SMEM)
LIMIT = pltpu.CompilerParams(vmem_limit_bytes=48 << 20)


def passed_along(shard, axis, by):
    size = lax.axis_size(axis)
    return lax.ppermute(shard, axis, [(i, (i + by) % size) for i in range(size)])


def rotated(chip, step, chips):
    return lax.rem(chip + step, chips)


def columns(head):
    return pl.ds(pl.multiple_of(head * HD, HD), HD)


def rows_of(block, size):
    return pl.ds(pl.multiple_of(block * size, size), size)


def pack_kernel(chips, chip_ref, *refs):
    sources, outs, sem = refs[:2], refs[2:-1], refs[-1]
    copies = [
        pltpu.make_async_copy(
            source.at[:, columns(rotated(chip_ref[0], step, chips))],
            outs[step].at[:, place * HD : (place + 1) * HD],
            sem.at[step * 2 + place],
        )
        for step in range(chips)
        for place, source in enumerate(sources)
    ]
    for copy in copies:
        copy.start()
    for copy in copies:
        copy.wait()


def grad_kernel(chips, chip_ref, grad_ref, weight_ref, query_ref, *outs):
    for step in range(chips):
        head = rotated(chip_ref[0], step, chips)
        outs[step][:, :HD] = query_ref[:, columns(head)]
        outs[step][:, HD:] = lax.dot_general(
            grad_ref[...],
            weight_ref[rows_of(head, HD), :],
            CONTRACT,
            preferred_element_type=jnp.float32,
        ).astype(jnp.bfloat16)


def assemble_kernel(chips, tokens, chip_ref, *refs):
    pieces, out_ref = refs[:chips], refs[chips]
    for step in range(chips):
        source = rotated(chip_ref[0], chips - step, chips)
        out_ref[rows_of(source, tokens), :] = pieces[step][...]


def turn_kernel(blocks, own_ref, other_ref, pair_ref, turned_ref):
    for side, source in enumerate((own_ref, other_ref)):
        pair_ref[side * blocks * BLOCK : (side + 1) * blocks * BLOCK] = source[...]
        for block in range(blocks):
            turned_ref[side * blocks + block] = jnp.transpose(
                source[block * BLOCK : (block + 1) * BLOCK, :HD]
            )


def attention_kernel(chips, tokens, scale, chip_ref, table_ref, count_ref, order_ref, *refs):
    pair_ref, turned_ref, pieces = refs[0], refs[1], refs[2 : 2 + chips]
    dq_ref, own_out, other_out, ask_buf, give_buf, total = refs[2 + chips :]
    blocks = chips * tokens // BLOCK
    half = blocks * BLOCK
    per_device = tokens // BLOCK
    zero = jnp.zeros((BLOCK, HD), jnp.bfloat16)
    for step in range(chips):
        source = rotated(chip_ref[0], chips - step, chips)
        for place in range(per_device):
            piece = pieces[step][place * BLOCK : (place + 1) * BLOCK, :]
            query, grad = piece[:, :HD], piece[:, HD:]
            block = source * per_device + place
            ask_buf[block, :BLOCK, :HD] = query
            ask_buf[block, :BLOCK, HD:] = zero
            ask_buf[block, BLOCK:, :HD] = zero
            ask_buf[block, BLOCK:, HD:] = grad
            give_buf[block, :BLOCK, :HD] = grad
            give_buf[block, :BLOCK, HD:] = zero
            give_buf[block, BLOCK:, :HD] = zero
            give_buf[block, BLOCK:, HD:] = query
    total[...] = jnp.zeros_like(total)

    def attend(block, count, width):
        index = [table_ref[block * NBR + slot] for slot in range(width)]
        slots = [rows_of(which, BLOCK) for which in index]
        pairs = jnp.concatenate([pair_ref[slot, :] for slot in slots], axis=0)
        both = lax.dot_general(pairs, ask_buf[block], CONTRACT, preferred_element_type=jnp.float32)
        scores, prob_grad = both[:, :BLOCK], both[:, BLOCK:]
        rest = (width - 1) * BLOCK
        last = jnp.where(count == width, scores[rest:], -jnp.inf)
        scores = jnp.concatenate([scores[:rest], last], axis=0) if rest else last
        peak = jnp.max(scores, axis=0, keepdims=True)
        weights = jnp.exp2((scores - peak) * (scale * math.log2(math.e)))
        probs = weights * (1.0 / jnp.sum(weights, axis=0, keepdims=True))
        half_probs = probs.astype(jnp.bfloat16)
        delta = jnp.sum(half_probs.astype(jnp.float32) * prob_grad, axis=0, keepdims=True)
        dscore = (probs * (prob_grad - delta)).astype(jnp.bfloat16)
        turned = jnp.concatenate([turned_ref[which] for which in index], axis=1)
        dq = jnp.dot(turned, dscore, preferred_element_type=jnp.float32)
        given = jnp.dot(
            jnp.concatenate([half_probs, dscore], axis=1),
            give_buf[block],
            preferred_element_type=jnp.float32,
        )
        dq_ref[rows_of(block, BLOCK), :] = jnp.transpose(dq * scale).astype(jnp.bfloat16)
        return slots, given

    def add(slots, given):
        for place, slot in enumerate(slots):
            total[slot, :] += given[place * BLOCK : (place + 1) * BLOCK]

    def two_blocks(pair, carry):
        block, mate = order_ref[2 * pair], order_ref[2 * pair + 1]
        count, other = count_ref[block], count_ref[mate]

        def work(width):
            first = attend(block, count, width)
            second = attend(mate, other, width)
            add(*first)
            add(*second)

        same = (count + 1) // 2 == (other + 1) // 2

        def alone(which, many):
            for width in WIDTHS:
                @pl.when((many > width - 2) & (many <= width))
                def _():
                    add(*attend(which, many, width))

        for width in WIDTHS:
            pl.when(same & (count > width - 2) & (count <= width))(functools.partial(work, width))

        @pl.when(jnp.logical_not(same))
        def _():
            alone(block, count)
            alone(mate, other)

        return carry

    lax.fori_loop(0, blocks // 2, two_blocks, 0)
    for part, out in ((slice(0, half), own_out), (slice(half, None), other_out)):
        out[:, :HD] = (total[part, HD:] * scale).astype(out.dtype)
        out[:, HD:] = total[part, :HD].astype(out.dtype)


def combine_kernel(chips, tokens, chip_ref, dq_ref, own_ref, other_ref, *outs):
    for step in range(chips):
        rows = rows_of(rotated(chip_ref[0], chips - step, chips), tokens)
        outs[step][:, :HD] = dq_ref[rows, :]
        outs[step][:, HD:] = (own_ref[rows, :] + other_ref[rows, :].astype(jnp.float32)).astype(
            jnp.bfloat16
        )


def project_kernel(chips, steps, chip_ref, *refs):
    pieces, weights = refs[: len(steps)], refs[len(steps) : len(steps) + 3]
    before, (out_ref, rows_buf, weight_buf) = refs[len(steps) + 3 : -3], refs[-3:]
    total = before[0][...] if before else None
    for place in range(3):
        for at, step in enumerate(steps):
            head = rotated(chip_ref[0], step, chips)
            rows_buf[place, :, at * HD : (at + 1) * HD] = pieces[at][
                :, place * HD : (place + 1) * HD
            ]
            weight_buf[place, :, at * HD : (at + 1) * HD] = weights[place][:, columns(head)]
        part = lax.dot_general(
            rows_buf[place], weight_buf[place], CONTRACT, preferred_element_type=jnp.float32
        )
        total = part if total is None else total + part
    out_ref[...] = total.astype(out_ref.dtype)


def head_per_chip(
    out_grad, query_act, key_act, value_act, out_weight, weights, neighbours, block_counts
):
    my_index = lax.axis_index("blk")
    chips = lax.axis_size("blk") // CORES
    tokens, features = query_act.shape
    scale = 1.0 / math.sqrt(HD)
    chip = (my_index // CORES).astype(jnp.int32).reshape(1)
    core = my_index % CORES
    per_device = tokens // BLOCK
    blocks = chips * per_device
    half = chips * tokens
    bf16 = functools.partial(jax.ShapeDtypeStruct, dtype=jnp.bfloat16)
    f32 = functools.partial(jax.ShapeDtypeStruct, dtype=jnp.float32)
    buf16 = functools.partial(pltpu.VMEM, dtype=jnp.bfloat16)
    buf32 = functools.partial(pltpu.VMEM, dtype=jnp.float32)

    def call(kernel, outs, scratch, scalars, *arrays, spec=VMEM):
        return pl.pallas_call(
            kernel,
            out_shape=outs,
            in_specs=[SMEM] * len(scalars) + [spec] * len(arrays),
            out_specs=jax.tree.map(lambda _: VMEM, outs),
            scratch_shapes=scratch,
            compiler_params=LIMIT,
        )(*scalars, *arrays)

    def by_chips(shard, step):
        pairs = [
            (CORES * c + k, CORES * ((c + step) % chips) + k)
            for c in range(chips)
            for k in range(CORES)
        ]
        return lax.ppermute(shard, "blk", pairs)

    def out_to(shards):
        return [shards[0]] + [by_chips(shards[step], step) for step in range(1, chips)]

    def across_cores(shard):
        return lax.ppermute(shard, "blk", [(i, i ^ 1) for i in range(chips * CORES)])

    own = neighbours.reshape(chips, CORES, per_device, NBR)
    own = lax.dynamic_index_in_dim(own, core, 1, keepdims=False)
    counts = block_counts.reshape(chips, CORES, per_device)
    counts = lax.dynamic_index_in_dim(counts, core, 1, keepdims=False).reshape(-1)
    holder = own // per_device
    table = (
        jnp.where(holder % CORES == core, 0, blocks)
        + (holder // CORES) * per_device
        + own % per_device
    ).reshape(-1)
    ids = jnp.arange(blocks, dtype=jnp.int32)
    rank_key = counts * blocks + ids
    rank = jnp.sum((rank_key[None, :] > rank_key[:, None]).astype(jnp.int32), axis=1)
    order = jnp.sum(jnp.where(rank[:, None] == ids[None, :], ids[:, None], 0), axis=0)

    args = functools.partial
    piece = [bf16((tokens, 2 * HD))] * chips
    pairs = call(
        args(pack_kernel, chips), piece, [pltpu.SemaphoreType.DMA((2 * chips,))],
        (chip,), key_act, value_act, spec=ANY,
    )
    pairs = out_to(pairs)
    asks = call(args(grad_kernel, chips), piece, [], (chip,), out_grad, out_weight, query_act)
    pairs, _ = lax.optimization_barrier((pairs, asks))
    asks = out_to(asks)
    own_pairs = call(
        args(assemble_kernel, chips, tokens), bf16((half, 2 * HD)), [], (chip,), *pairs
    )
    other_pairs = across_cores(own_pairs)
    both_pairs, turned = call(
        args(turn_kernel, blocks), [bf16((2 * half, 2 * HD)), bf16((2 * blocks, HD, BLOCK))], [],
        (), own_pairs, other_pairs,
    )
    dq, own_part, sent_part = call(
        args(attention_kernel, chips, tokens, scale),
        [bf16((half, HD)), f32((half, 2 * HD)), bf16((half, 2 * HD))],
        [
            buf16((blocks, 2 * BLOCK, 2 * HD)),
            buf16((blocks, 2 * BLOCK, 2 * HD)),
            buf32((2 * half, 2 * HD)),
        ],
        (chip, table, counts, order), both_pairs, turned, *asks,
    )
    came_part = across_cores(sent_part)
    back = call(
        args(combine_kernel, chips, tokens), [bf16((tokens, 3 * HD))] * chips, [],
        (chip,), dq, own_part, came_part,
    )
    back = [back[0]] + [by_chips(back[step], chips - step) for step in range(1, chips)]
    near = [min(step, chips - step) * 4 <= chips for step in range(chips)]
    early = [step for step in range(chips) if near[step]]
    late = [step for step in range(chips) if not near[step]]

    def project(steps, outs, *before):
        return call(
            args(project_kernel, chips, steps), outs,
            [buf16((3, tokens, len(steps) * HD)), buf16((3, features, len(steps) * HD))],
            (chip,), *(back[step] for step in steps), *weights, *before,
        )

    return project(late, bf16((tokens, features)), project(early, f32((tokens, features))))


def by_window(
    out_grad, query_act, key_act, value_act, out_weight, weights, neighbours, block_counts
):
    cycle_size = lax.axis_size("blk")
    my_index = lax.axis_index("blk")
    tokens, features = query_act.shape
    head_count = features // HD
    query_blocks = tokens // BLOCK
    reach_dev = (WIN + query_blocks - 1) // query_blocks
    total_blocks = query_blocks * cycle_size
    window_blocks = (2 * reach_dev + 1) * query_blocks
    scale = 1.0 / math.sqrt(HD)
    attn_grad = lax.dot_general(
        lax.all_gather(out_grad, "sp", axis=0, tiled=True),
        out_weight,
        CONTRACT,
        preferred_element_type=jnp.float32,
    ).astype(jnp.bfloat16)
    key_value = jnp.stack((key_act, value_act))
    gathered = jnp.concatenate(
        [
            key_value if offset == 0 else passed_along(key_value, "blk", -offset)
            for offset in range(-reach_dev, reach_dev + 1)
        ],
        axis=1,
    ).reshape(2, window_blocks, BLOCK, features)
    anchor = (my_index - reach_dev) * query_blocks
    own_lists = lax.dynamic_slice_in_dim(neighbours, my_index * query_blocks, query_blocks, 0)
    own_counts = lax.dynamic_slice_in_dim(block_counts, my_index * query_blocks, query_blocks, 0)
    window_index = ((own_lists - anchor) % total_blocks).reshape(-1)
    picked = jnp.concatenate(
        [
            lax.dynamic_slice_in_dim(gathered, window_index[n], 1, 1)
            for n in range(query_blocks * NBR)
        ],
        axis=1,
    ).reshape(2, query_blocks, NBR, BLOCK, head_count, HD)
    query_heads = query_act.reshape(query_blocks, BLOCK, head_count, HD)
    grad_heads = attn_grad.reshape(query_blocks, BLOCK, head_count, HD)
    einsum = functools.partial(jnp.einsum, preferred_element_type=jnp.float32)
    scores = scale * einsum("bihd,bsjhd->bhisj", query_heads, picked[0])
    live_slots = jnp.arange(NBR)[None, :] < own_counts[:, None]
    scores = jnp.where(live_slots[:, None, None, :, None], scores, -jnp.inf)
    row_peak = jnp.max(scores, axis=(3, 4), keepdims=True)
    log_total = row_peak + jnp.log(jnp.sum(jnp.exp(scores - row_peak), axis=(3, 4), keepdims=True))
    soft_probs = jnp.exp(scores - log_total)
    probs_half = soft_probs.astype(jnp.bfloat16)
    outputs = einsum("bhisj,bsjhd->bihd", probs_half, picked[1])
    row_delta = jnp.transpose(jnp.sum(grad_heads.astype(jnp.float32) * outputs, axis=3), (0, 2, 1))
    prob_grad = einsum("bihd,bsjhd->bhisj", grad_heads, picked[1])
    dscore_half = (soft_probs * (prob_grad - row_delta[:, :, :, None, None])).astype(jnp.bfloat16)
    query_grad = scale * einsum("bhisj,bsjhd->bihd", dscore_half, picked[0])
    query_grad = query_grad.astype(jnp.bfloat16).reshape(tokens, features)
    key_slots = scale * einsum("bhisj,bihd->bsjhd", dscore_half, query_heads)
    value_slots = einsum("bhisj,bihd->bsjhd", probs_half, grad_heads)
    slot_grads = jnp.stack((key_slots, value_slots)).reshape(
        2, query_blocks * NBR, BLOCK * features
    )
    selector = (jnp.arange(window_blocks)[:, None] == window_index.reshape(1, -1)).astype(
        jnp.float32
    )
    window_grads = jnp.einsum("wn,gnc->gwc", selector, slot_grads, precision=lax.Precision.HIGHEST)
    summed = 0.0
    for offset in range(-reach_dev, reach_dev + 1):
        first = (offset + reach_dev) * query_blocks
        portion = window_grads[:, first : first + query_blocks]
        summed = summed + (portion if offset == 0 else passed_along(portion, "blk", offset))
    own_grads = summed.reshape(2, tokens, features).astype(jnp.bfloat16)
    summed_rows = 0.0
    for grad, weight in zip((query_grad, own_grads[0], own_grads[1]), weights, strict=True):
        summed_rows = summed_rows + lax.dot_general(
            grad, weight, CONTRACT, preferred_element_type=jnp.float32
        )
    input_grad = lax.psum_scatter(summed_rows, "sp", scatter_dimension=0, tiled=True)
    return input_grad.astype(jnp.bfloat16)


def body(
    out_grad,
    query_act,
    key_act,
    value_act,
    out_weight,
    query_weight,
    key_weight,
    value_weight,
    neighbours,
    block_counts,
):
    heads = query_act.shape[1] // HD
    one_head = lax.axis_size("sp") == 1 and lax.axis_size("blk") == heads * CORES
    return (head_per_chip if one_head else by_window)(
        out_grad,
        query_act,
        key_act,
        value_act,
        out_weight,
        (query_weight, key_weight, value_weight),
        neighbours,
        block_counts,
    )


def solution(mesh):
    return jax.shard_map(
        body,
        mesh=mesh,
        in_specs=(
            P(("groups", "blk", "sp"), None),
            P(("groups", "blk"), "sp"),
            P(("groups", "blk"), "sp"),
            P(("groups", "blk"), "sp"),
            P("sp", None),
            P(None, "sp"),
            P(None, "sp"),
            P(None, "sp"),
            P("groups", None),
            P("groups"),
        ),
        out_specs=P(("groups", "blk", "sp"), None),
        check_vma=False,
    )
```

```python
import functools
import math

import jax
import jax.numpy as jnp
from jax import lax
from jax.experimental import pallas as pl
from jax.experimental.pallas import tpu as pltpu
from jax.sharding import PartitionSpec as P

HD = 128
BLOCK = 128
NBR = 8
WIN = 8
CORES = 2
WIDTHS = (2, 4, 6, 8)
GROUP = 4
CONTRACT = (((1,), (1,)), ((), ()))
ANY = pl.BlockSpec(memory_space=pl.ANY)
VMEM = pl.BlockSpec(memory_space=pltpu.VMEM)
SMEM = pl.BlockSpec(memory_space=pltpu.SMEM)
LIMIT = pltpu.CompilerParams(vmem_limit_bytes=48 << 20)


def passed_along(shard, axis, by):
    size = lax.axis_size(axis)
    return lax.ppermute(shard, axis, [(i, (i + by) % size) for i in range(size)])


def rotated(chip, step, chips):
    return lax.rem(chip + step, chips)


def columns(head):
    return pl.ds(pl.multiple_of(head * HD, HD), HD)


def rows_of(block, size):
    return pl.ds(pl.multiple_of(block * size, size), size)


def pack_kernel(chips, chip_ref, *refs):
    sources, outs, sem = refs[:2], refs[2:-1], refs[-1]
    copies = [
        pltpu.make_async_copy(
            source.at[:, columns(rotated(chip_ref[0], step, chips))],
            outs[step].at[:, place * HD : (place + 1) * HD],
            sem.at[step * 2 + place],
        )
        for step in range(chips)
        for place, source in enumerate(sources)
    ]
    for copy in copies:
        copy.start()
    for copy in copies:
        copy.wait()


def grad_kernel(chips, chip_ref, grad_ref, weight_ref, query_ref, *outs):
    for step in range(chips):
        head = rotated(chip_ref[0], step, chips)
        outs[step][:, :HD] = query_ref[:, columns(head)]
        outs[step][:, HD:] = lax.dot_general(
            grad_ref[...],
            weight_ref[rows_of(head, HD), :],
            CONTRACT,
            preferred_element_type=jnp.float32,
        ).astype(jnp.bfloat16)


def assemble_kernel(chips, tokens, chip_ref, *refs):
    pieces, out_ref = refs[:chips], refs[chips]
    for step in range(chips):
        source = rotated(chip_ref[0], chips - step, chips)
        out_ref[rows_of(source, tokens), :] = pieces[step][...]


def turn_kernel(blocks, own_ref, other_ref, pair_ref, turned_ref):
    for side, source in enumerate((own_ref, other_ref)):
        pair_ref[side * blocks * BLOCK : (side + 1) * blocks * BLOCK] = source[...]
        for block in range(blocks):
            turned_ref[side * blocks + block] = jnp.transpose(
                source[block * BLOCK : (block + 1) * BLOCK, :HD]
            )


def attention_kernel(chips, tokens, scale, chip_ref, table_ref, count_ref, order_ref, *refs):
    pair_ref, turned_ref, pieces = refs[0], refs[1], refs[2 : 2 + chips]
    dq_ref, total, sent_out, ask_buf, give_buf = refs[2 + chips :]
    blocks = chips * tokens // BLOCK
    half = blocks * BLOCK
    per_device = tokens // BLOCK
    ask_buf[...] = jnp.zeros_like(ask_buf)
    give_buf[...] = jnp.zeros_like(give_buf)
    for step in range(chips):
        source = rotated(chip_ref[0], chips - step, chips)
        for place in range(per_device):
            piece = pieces[step][place * BLOCK : (place + 1) * BLOCK, :]
            query, grad = piece[:, :HD], piece[:, HD:]
            block = source * per_device + place
            ask_buf[block, :HD, :BLOCK] = jnp.transpose(query)
            ask_buf[block, HD:, BLOCK:] = jnp.transpose(grad)
            give_buf[block, :BLOCK, :HD] = grad
            give_buf[block, BLOCK:, HD:] = query
    total[...] = jnp.zeros_like(total)

    def attend(block, width):
        count = count_ref[block]
        index = [table_ref[block * NBR + slot] for slot in range(width)]
        slots = [rows_of(which, BLOCK) for which in index]
        pairs = jnp.concatenate([pair_ref[slot, :] for slot in slots], axis=0)
        both = jnp.dot(pairs, ask_buf[block], preferred_element_type=jnp.float32)
        scores, prob_grad = both[:, :BLOCK], both[:, BLOCK:]
        scores = jnp.concatenate(
            [
                jnp.where(slot < count, scores[slot * BLOCK : (slot + 1) * BLOCK], -jnp.inf)
                for slot in range(width)
            ],
            axis=0,
        )
        peak = jnp.max(scores, axis=0, keepdims=True)
        weights = jnp.exp2((scores - peak) * (scale * math.log2(math.e)))
        probs = weights * (1.0 / jnp.sum(weights, axis=0, keepdims=True))
        half_probs = probs.astype(jnp.bfloat16)
        delta = jnp.sum(half_probs.astype(jnp.float32) * prob_grad, axis=0, keepdims=True)
        dscore = (probs * (prob_grad - delta)).astype(jnp.bfloat16)
        turned = jnp.concatenate([turned_ref[which] for which in index], axis=1)
        dq = jnp.dot(turned, dscore, preferred_element_type=jnp.float32)
        given = jnp.dot(
            jnp.concatenate([half_probs, dscore], axis=1),
            give_buf[block],
            preferred_element_type=jnp.float32,
        )
        dq_ref[rows_of(block, BLOCK), :] = jnp.transpose(dq * scale).astype(jnp.bfloat16)
        return slots, given

    def one_group(group, carry):
        members = [order_ref[group * GROUP + member] for member in range(GROUP)]
        most = count_ref[members[0]]

        def work(width):
            for slots, given in [attend(member, width) for member in members]:
                for place, slot in enumerate(slots):
                    total[slot, :] += given[place * BLOCK : (place + 1) * BLOCK]

        below = 0
        for width in WIDTHS:
            pl.when((most > below) & (most <= width))(functools.partial(work, width))
            below = width
        return carry

    lax.fori_loop(0, blocks // GROUP, one_group, 0)
    sent_out[...] = total[half:].astype(jnp.bfloat16)


def combine_kernel(chips, tokens, scale, chip_ref, dq_ref, own_ref, other_ref, *outs):
    for step in range(chips):
        rows = rows_of(rotated(chip_ref[0], chips - step, chips), tokens)
        outs[step][:, :HD] = dq_ref[rows, :]
        summed = own_ref[rows, :] + other_ref[rows, :].astype(jnp.float32)
        outs[step][:, HD : 2 * HD] = (summed[:, HD:] * scale).astype(jnp.bfloat16)
        outs[step][:, 2 * HD :] = summed[:, :HD].astype(jnp.bfloat16)


def project_kernel(chips, steps, chip_ref, *refs):
    pieces, weights = refs[: len(steps)], refs[len(steps) : len(steps) + 3]
    before, (out_ref, rows_buf, weight_buf) = refs[len(steps) + 3 : -3], refs[-3:]
    total = before[0][...] if before else None
    for place in range(3):
        for at, step in enumerate(steps):
            head = rotated(chip_ref[0], step, chips)
            rows_buf[place, :, at * HD : (at + 1) * HD] = pieces[at][
                :, place * HD : (place + 1) * HD
            ]
            weight_buf[place, :, at * HD : (at + 1) * HD] = weights[place][:, columns(head)]
        part = lax.dot_general(
            rows_buf[place], weight_buf[place], CONTRACT, preferred_element_type=jnp.float32
        )
        total = part if total is None else total + part
    out_ref[...] = total.astype(out_ref.dtype)


def head_per_chip(
    out_grad, query_act, key_act, value_act, out_weight, weights, neighbours, block_counts
):
    my_index = lax.axis_index("blk")
    chips = lax.axis_size("blk") // CORES
    tokens, features = query_act.shape
    scale = 1.0 / math.sqrt(HD)
    chip = (my_index // CORES).astype(jnp.int32).reshape(1)
    core = my_index % CORES
    per_device = tokens // BLOCK
    blocks = chips * per_device
    half = chips * tokens
    bf16 = functools.partial(jax.ShapeDtypeStruct, dtype=jnp.bfloat16)
    f32 = functools.partial(jax.ShapeDtypeStruct, dtype=jnp.float32)
    buf16 = functools.partial(pltpu.VMEM, dtype=jnp.bfloat16)

    def call(kernel, outs, scratch, scalars, *arrays, spec=VMEM):
        return pl.pallas_call(
            kernel,
            out_shape=outs,
            in_specs=[SMEM] * len(scalars) + [spec] * len(arrays),
            out_specs=jax.tree.map(lambda _: VMEM, outs),
            scratch_shapes=scratch,
            compiler_params=LIMIT,
        )(*scalars, *arrays)

    def by_chips(shard, step):
        pairs = [
            (CORES * c + k, CORES * ((c + step) % chips) + k)
            for c in range(chips)
            for k in range(CORES)
        ]
        return lax.ppermute(shard, "blk", pairs)

    def out_to(shards):
        return [shards[0]] + [by_chips(shards[step], step) for step in range(1, chips)]

    def across_cores(shard):
        return lax.ppermute(shard, "blk", [(i, i ^ 1) for i in range(chips * CORES)])

    own = neighbours.reshape(chips, CORES, per_device, NBR)
    own = lax.dynamic_index_in_dim(own, core, 1, keepdims=False)
    counts = block_counts.reshape(chips, CORES, per_device)
    counts = lax.dynamic_index_in_dim(counts, core, 1, keepdims=False).reshape(-1)
    holder = own // per_device
    table = (
        jnp.where(holder % CORES == core, 0, blocks)
        + (holder // CORES) * per_device
        + own % per_device
    ).reshape(-1)
    ids = jnp.arange(blocks, dtype=jnp.int32)
    rank_key = counts * blocks + ids
    rank = jnp.sum((rank_key[None, :] > rank_key[:, None]).astype(jnp.int32), axis=1)
    order = jnp.sum(jnp.where(rank[:, None] == ids[None, :], ids[:, None], 0), axis=0)

    args = functools.partial
    piece = [bf16((tokens, 2 * HD))] * chips
    pairs = call(
        args(pack_kernel, chips), piece, [pltpu.SemaphoreType.DMA((2 * chips,))],
        (chip,), key_act, value_act, spec=ANY,
    )
    pairs = out_to(pairs)
    asks = call(args(grad_kernel, chips), piece, [], (chip,), out_grad, out_weight, query_act)
    pairs, _ = lax.optimization_barrier((pairs, asks))
    asks = out_to(asks)
    own_pairs = call(
        args(assemble_kernel, chips, tokens), bf16((half, 2 * HD)), [], (chip,), *pairs
    )
    other_pairs = across_cores(own_pairs)
    both_pairs, turned = call(
        args(turn_kernel, blocks), [bf16((2 * half, 2 * HD)), bf16((2 * blocks, HD, BLOCK))], [],
        (), own_pairs, other_pairs,
    )
    dq, own_part, sent_part = call(
        args(attention_kernel, chips, tokens, scale),
        [bf16((half, HD)), f32((2 * half, 2 * HD)), bf16((half, 2 * HD))],
        [
            buf16((blocks, 2 * HD, 2 * BLOCK)),
            buf16((blocks, 2 * BLOCK, 2 * HD)),
        ],
        (chip, table, counts, order), both_pairs, turned, *asks,
    )
    came_part = across_cores(sent_part)
    back = call(
        args(combine_kernel, chips, tokens, scale), [bf16((tokens, 3 * HD))] * chips, [],
        (chip,), dq, own_part, came_part,
    )
    back = [back[0]] + [by_chips(back[step], chips - step) for step in range(1, chips)]
    near = [min(step, chips - step) * 4 <= chips for step in range(chips)]
    early = [step for step in range(chips) if near[step]]
    late = [step for step in range(chips) if not near[step]]

    def project(steps, outs, *before):
        return call(
            args(project_kernel, chips, steps), outs,
            [buf16((3, tokens, len(steps) * HD)), buf16((3, features, len(steps) * HD))],
            (chip,), *(back[step] for step in steps), *weights, *before,
        )

    return project(late, bf16((tokens, features)), project(early, f32((tokens, features))))


def by_window(
    out_grad, query_act, key_act, value_act, out_weight, weights, neighbours, block_counts
):
    cycle_size = lax.axis_size("blk")
    my_index = lax.axis_index("blk")
    tokens, features = query_act.shape
    head_count = features // HD
    query_blocks = tokens // BLOCK
    reach_dev = (WIN + query_blocks - 1) // query_blocks
    total_blocks = query_blocks * cycle_size
    window_blocks = (2 * reach_dev + 1) * query_blocks
    scale = 1.0 / math.sqrt(HD)
    attn_grad = lax.dot_general(
        lax.all_gather(out_grad, "sp", axis=0, tiled=True),
        out_weight,
        CONTRACT,
        preferred_element_type=jnp.float32,
    ).astype(jnp.bfloat16)
    key_value = jnp.stack((key_act, value_act))
    gathered = jnp.concatenate(
        [
            key_value if offset == 0 else passed_along(key_value, "blk", -offset)
            for offset in range(-reach_dev, reach_dev + 1)
        ],
        axis=1,
    ).reshape(2, window_blocks, BLOCK, features)
    anchor = (my_index - reach_dev) * query_blocks
    own_lists = lax.dynamic_slice_in_dim(neighbours, my_index * query_blocks, query_blocks, 0)
    own_counts = lax.dynamic_slice_in_dim(block_counts, my_index * query_blocks, query_blocks, 0)
    window_index = ((own_lists - anchor) % total_blocks).reshape(-1)
    picked = jnp.concatenate(
        [
            lax.dynamic_slice_in_dim(gathered, window_index[n], 1, 1)
            for n in range(query_blocks * NBR)
        ],
        axis=1,
    ).reshape(2, query_blocks, NBR, BLOCK, head_count, HD)
    query_heads = query_act.reshape(query_blocks, BLOCK, head_count, HD)
    grad_heads = attn_grad.reshape(query_blocks, BLOCK, head_count, HD)
    einsum = functools.partial(jnp.einsum, preferred_element_type=jnp.float32)
    scores = scale * einsum("bihd,bsjhd->bhisj", query_heads, picked[0])
    live_slots = jnp.arange(NBR)[None, :] < own_counts[:, None]
    scores = jnp.where(live_slots[:, None, None, :, None], scores, -jnp.inf)
    row_peak = jnp.max(scores, axis=(3, 4), keepdims=True)
    log_total = row_peak + jnp.log(jnp.sum(jnp.exp(scores - row_peak), axis=(3, 4), keepdims=True))
    soft_probs = jnp.exp(scores - log_total)
    probs_half = soft_probs.astype(jnp.bfloat16)
    outputs = einsum("bhisj,bsjhd->bihd", probs_half, picked[1])
    row_delta = jnp.transpose(jnp.sum(grad_heads.astype(jnp.float32) * outputs, axis=3), (0, 2, 1))
    prob_grad = einsum("bihd,bsjhd->bhisj", grad_heads, picked[1])
    dscore_half = (soft_probs * (prob_grad - row_delta[:, :, :, None, None])).astype(jnp.bfloat16)
    query_grad = scale * einsum("bhisj,bsjhd->bihd", dscore_half, picked[0])
    query_grad = query_grad.astype(jnp.bfloat16).reshape(tokens, features)
    key_slots = scale * einsum("bhisj,bihd->bsjhd", dscore_half, query_heads)
    value_slots = einsum("bhisj,bihd->bsjhd", probs_half, grad_heads)
    slot_grads = jnp.stack((key_slots, value_slots)).reshape(
        2, query_blocks * NBR, BLOCK * features
    )
    selector = (jnp.arange(window_blocks)[:, None] == window_index.reshape(1, -1)).astype(
        jnp.float32
    )
    window_grads = jnp.einsum("wn,gnc->gwc", selector, slot_grads, precision=lax.Precision.HIGHEST)
    summed = 0.0
    for offset in range(-reach_dev, reach_dev + 1):
        first = (offset + reach_dev) * query_blocks
        portion = window_grads[:, first : first + query_blocks]
        summed = summed + (portion if offset == 0 else passed_along(portion, "blk", offset))
    own_grads = summed.reshape(2, tokens, features).astype(jnp.bfloat16)
    summed_rows = 0.0
    for grad, weight in zip((query_grad, own_grads[0], own_grads[1]), weights, strict=True):
        summed_rows = summed_rows + lax.dot_general(
            grad, weight, CONTRACT, preferred_element_type=jnp.float32
        )
    input_grad = lax.psum_scatter(summed_rows, "sp", scatter_dimension=0, tiled=True)
    return input_grad.astype(jnp.bfloat16)


def body(
    out_grad,
    query_act,
    key_act,
    value_act,
    out_weight,
    query_weight,
    key_weight,
    value_weight,
    neighbours,
    block_counts,
):
    heads = query_act.shape[1] // HD
    one_head = lax.axis_size("sp") == 1 and lax.axis_size("blk") == heads * CORES
    return (head_per_chip if one_head else by_window)(
        out_grad,
        query_act,
        key_act,
        value_act,
        out_weight,
        (query_weight, key_weight, value_weight),
        neighbours,
        block_counts,
    )


def solution(mesh):
    return jax.shard_map(
        body,
        mesh=mesh,
        in_specs=(
            P(("groups", "blk", "sp"), None),
            P(("groups", "blk"), "sp"),
            P(("groups", "blk"), "sp"),
            P(("groups", "blk"), "sp"),
            P("sp", None),
            P(None, "sp"),
            P(None, "sp"),
            P(None, "sp"),
            P("groups", None),
            P("groups"),
        ),
        out_specs=P(("groups", "blk", "sp"), None),
        check_vma=False,
    )
```

```python
import functools
import math

import jax
import jax.numpy as jnp
from jax import lax
from jax.experimental import pallas as pl
from jax.experimental.pallas import tpu as pltpu
from jax.sharding import PartitionSpec as P

HD = 128
BLOCK = 128
NBR = 8
WIN = 8
CORES = 2
WIDTHS = (2, 4, 6, 8)
GROUP = 4
CONTRACT = (((1,), (1,)), ((), ()))
ANY = pl.BlockSpec(memory_space=pl.ANY)
VMEM = pl.BlockSpec(memory_space=pltpu.VMEM)
SMEM = pl.BlockSpec(memory_space=pltpu.SMEM)
LIMIT = pltpu.CompilerParams(vmem_limit_bytes=30 << 20)


def passed_along(shard, axis, by):
    size = lax.axis_size(axis)
    return lax.ppermute(shard, axis, [(i, (i + by) % size) for i in range(size)])


def rotated(chip, step, chips):
    return lax.rem(chip + step, chips)


def columns(head):
    return pl.ds(pl.multiple_of(head * HD, HD), HD)


def rows_of(block, size):
    return pl.ds(pl.multiple_of(block * size, size), size)


def pack_kernel(chips, chip_ref, *refs):
    sources, outs, sem = refs[:2], refs[2:-1], refs[-1]
    copies = [
        pltpu.make_async_copy(
            source.at[:, columns(rotated(chip_ref[0], step, chips))],
            outs[step].at[:, place * HD : (place + 1) * HD],
            sem.at[step * 2 + place],
        )
        for step in range(chips)
        for place, source in enumerate(sources)
    ]
    for copy in copies:
        copy.start()
    for copy in copies:
        copy.wait()


def grad_kernel(chips, chip_ref, grad_ref, weight_ref, query_ref, *outs):
    for step in range(chips):
        head = rotated(chip_ref[0], step, chips)
        outs[step][:, :HD] = query_ref[:, columns(head)]
        outs[step][:, HD:] = lax.dot_general(
            grad_ref[...],
            weight_ref[rows_of(head, HD), :],
            CONTRACT,
            preferred_element_type=jnp.float32,
        ).astype(jnp.bfloat16)


def assemble_kernel(chips, tokens, chip_ref, *refs):
    pieces, out_ref = refs[:chips], refs[chips]
    for step in range(chips):
        source = rotated(chip_ref[0], chips - step, chips)
        out_ref[rows_of(source, tokens), :] = pieces[step][...]


def turn_kernel(blocks, own_ref, other_ref, pair_ref, turned_ref):
    for side, source in enumerate((own_ref, other_ref)):
        pair_ref[side * blocks * BLOCK : (side + 1) * blocks * BLOCK] = source[...]
        for block in range(blocks):
            turned_ref[side * blocks + block] = jnp.transpose(
                source[block * BLOCK : (block + 1) * BLOCK, :HD]
            )


def attention_kernel(chips, tokens, scale, chip_ref, table_ref, count_ref, order_ref, *refs):
    pair_ref, turned_ref, pieces = refs[0], refs[1], refs[2 : 2 + chips]
    dq_ref, total, sent_out, ask_buf, give_buf = refs[2 + chips :]
    blocks = chips * tokens // BLOCK
    half = blocks * BLOCK
    per_device = tokens // BLOCK
    ask_buf[...] = jnp.zeros_like(ask_buf)
    give_buf[...] = jnp.zeros_like(give_buf)
    for step in range(chips):
        source = rotated(chip_ref[0], chips - step, chips)
        for place in range(per_device):
            piece = pieces[step][place * BLOCK : (place + 1) * BLOCK, :]
            query, grad = piece[:, :HD], piece[:, HD:]
            block = source * per_device + place
            ask_buf[block, :HD, :BLOCK] = jnp.transpose(query)
            ask_buf[block, HD:, BLOCK:] = jnp.transpose(grad)
            give_buf[block, :BLOCK, :HD] = grad
            give_buf[block, BLOCK:, HD:] = query
    total[...] = jnp.zeros_like(total)

    def attend(block, width):
        count = count_ref[block]
        index = [table_ref[block * NBR + slot] for slot in range(width)]
        slots = [rows_of(which, BLOCK) for which in index]
        pairs = jnp.concatenate([pair_ref[slot, :] for slot in slots], axis=0)
        both = jnp.dot(pairs, ask_buf[block], preferred_element_type=jnp.float32)
        scores, prob_grad = both[:, :BLOCK], both[:, BLOCK:]
        scores = jnp.concatenate(
            [
                jnp.where(slot < count, scores[slot * BLOCK : (slot + 1) * BLOCK], -jnp.inf)
                for slot in range(width)
            ],
            axis=0,
        )
        peak = jnp.max(scores, axis=0, keepdims=True)
        weights = jnp.exp2((scores - peak) * (scale * math.log2(math.e)))
        probs = weights * (1.0 / jnp.sum(weights, axis=0, keepdims=True))
        half_probs = probs.astype(jnp.bfloat16)
        delta = jnp.sum(half_probs.astype(jnp.float32) * prob_grad, axis=0, keepdims=True)
        dscore = (probs * (prob_grad - delta)).astype(jnp.bfloat16)
        turned = jnp.concatenate([turned_ref[which] for which in index], axis=1)
        dq = jnp.dot(turned, dscore, preferred_element_type=jnp.float32)
        given = jnp.dot(
            jnp.concatenate([half_probs, dscore], axis=1),
            give_buf[block],
            preferred_element_type=jnp.float32,
        )
        dq_ref[rows_of(block, BLOCK), :] = jnp.transpose(dq * scale).astype(jnp.bfloat16)
        return slots, given

    def one_group(group, carry):
        members = [order_ref[group * GROUP + member] for member in range(GROUP)]
        most = count_ref[members[0]]

        def work(width):
            for slots, given in [attend(member, width) for member in members]:
                for place, slot in enumerate(slots):
                    total[slot, :] += given[place * BLOCK : (place + 1) * BLOCK]

        below = 0
        for width in WIDTHS:
            pl.when((most > below) & (most <= width))(functools.partial(work, width))
            below = width
        return carry

    lax.fori_loop(0, blocks // GROUP, one_group, 0)
    sent_out[...] = total[half:].astype(jnp.bfloat16)


def combine_kernel(chips, tokens, scale, chip_ref, dq_ref, own_ref, other_ref, *outs):
    for step in range(chips):
        rows = rows_of(rotated(chip_ref[0], chips - step, chips), tokens)
        outs[step][:, :HD] = dq_ref[rows, :]
        summed = own_ref[rows, :] + other_ref[rows, :].astype(jnp.float32)
        outs[step][:, HD : 2 * HD] = (summed[:, HD:] * scale).astype(jnp.bfloat16)
        outs[step][:, 2 * HD :] = summed[:, :HD].astype(jnp.bfloat16)


def project_kernel(chips, steps, chip_ref, *refs):
    pieces, weights = refs[: len(steps)], refs[len(steps) : len(steps) + 3]
    before, (out_ref, rows_buf, weight_buf) = refs[len(steps) + 3 : -3], refs[-3:]
    total = before[0][...] if before else None
    for place in range(3):
        for at, step in enumerate(steps):
            head = rotated(chip_ref[0], step, chips)
            rows_buf[place, :, at * HD : (at + 1) * HD] = pieces[at][
                :, place * HD : (place + 1) * HD
            ]
            weight_buf[place, :, at * HD : (at + 1) * HD] = weights[place][:, columns(head)]
        part = lax.dot_general(
            rows_buf[place], weight_buf[place], CONTRACT, preferred_element_type=jnp.float32
        )
        total = part if total is None else total + part
    out_ref[...] = total.astype(out_ref.dtype)


def head_per_chip(
    out_grad, query_act, key_act, value_act, out_weight, weights, neighbours, block_counts
):
    my_index = lax.axis_index("blk")
    chips = lax.axis_size("blk") // CORES
    tokens, features = query_act.shape
    scale = 1.0 / math.sqrt(HD)
    chip = (my_index // CORES).astype(jnp.int32).reshape(1)
    core = my_index % CORES
    per_device = tokens // BLOCK
    blocks = chips * per_device
    half = chips * tokens
    bf16 = functools.partial(jax.ShapeDtypeStruct, dtype=jnp.bfloat16)
    f32 = functools.partial(jax.ShapeDtypeStruct, dtype=jnp.float32)
    buf16 = functools.partial(pltpu.VMEM, dtype=jnp.bfloat16)

    def call(kernel, outs, scratch, scalars, *arrays, spec=VMEM):
        return pl.pallas_call(
            kernel,
            out_shape=outs,
            in_specs=[SMEM] * len(scalars) + [spec] * len(arrays),
            out_specs=jax.tree.map(lambda _: VMEM, outs),
            scratch_shapes=scratch,
            compiler_params=LIMIT,
        )(*scalars, *arrays)

    def by_chips(shard, step):
        pairs = [
            (CORES * c + k, CORES * ((c + step) % chips) + k)
            for c in range(chips)
            for k in range(CORES)
        ]
        return lax.ppermute(shard, "blk", pairs)

    def out_to(shards):
        return [shards[0]] + [by_chips(shards[step], step) for step in range(1, chips)]

    def across_cores(shard):
        return lax.ppermute(shard, "blk", [(i, i ^ 1) for i in range(chips * CORES)])

    own = neighbours.reshape(chips, CORES, per_device, NBR)
    own = lax.dynamic_index_in_dim(own, core, 1, keepdims=False)
    counts = block_counts.reshape(chips, CORES, per_device)
    counts = lax.dynamic_index_in_dim(counts, core, 1, keepdims=False).reshape(-1)
    holder = own // per_device
    table = (
        jnp.where(holder % CORES == core, 0, blocks)
        + (holder // CORES) * per_device
        + own % per_device
    ).reshape(-1)
    ids = jnp.arange(blocks, dtype=jnp.int32)
    rank_key = counts * blocks + ids
    rank = jnp.sum((rank_key[None, :] > rank_key[:, None]).astype(jnp.int32), axis=1)
    order = jnp.sum(jnp.where(rank[:, None] == ids[None, :], ids[:, None], 0), axis=0)

    args = functools.partial
    piece = [bf16((tokens, 2 * HD))] * chips
    pairs = call(
        args(pack_kernel, chips), piece, [pltpu.SemaphoreType.DMA((2 * chips,))],
        (chip,), key_act, value_act, spec=ANY,
    )
    pairs = out_to(pairs)
    asks = call(args(grad_kernel, chips), piece, [], (chip,), out_grad, out_weight, query_act)
    pairs, _ = lax.optimization_barrier((pairs, asks))
    asks = out_to(asks)
    own_pairs = call(
        args(assemble_kernel, chips, tokens), bf16((half, 2 * HD)), [], (chip,), *pairs
    )
    other_pairs = across_cores(own_pairs)
    both_pairs, turned = call(
        args(turn_kernel, blocks), [bf16((2 * half, 2 * HD)), bf16((2 * blocks, HD, BLOCK))], [],
        (), own_pairs, other_pairs,
    )
    dq, own_part, sent_part = call(
        args(attention_kernel, chips, tokens, scale),
        [bf16((half, HD)), f32((2 * half, 2 * HD)), bf16((half, 2 * HD))],
        [
            buf16((blocks, 2 * HD, 2 * BLOCK)),
            buf16((blocks, 2 * BLOCK, 2 * HD)),
        ],
        (chip, table, counts, order), both_pairs, turned, *asks,
    )
    came_part = across_cores(sent_part)
    back = call(
        args(combine_kernel, chips, tokens, scale), [bf16((tokens, 3 * HD))] * chips, [],
        (chip,), dq, own_part, came_part,
    )
    back = [back[0]] + [by_chips(back[step], chips - step) for step in range(1, chips)]
    near = [min(step, chips - step) * 4 <= chips for step in range(chips)]
    early = [step for step in range(chips) if near[step]]
    late = [step for step in range(chips) if not near[step]]

    def project(steps, outs, *before):
        return call(
            args(project_kernel, chips, steps), outs,
            [buf16((3, tokens, len(steps) * HD)), buf16((3, features, len(steps) * HD))],
            (chip,), *(back[step] for step in steps), *weights, *before,
        )

    return project(late, bf16((tokens, features)), project(early, f32((tokens, features))))


def by_window(
    out_grad, query_act, key_act, value_act, out_weight, weights, neighbours, block_counts
):
    cycle_size = lax.axis_size("blk")
    my_index = lax.axis_index("blk")
    tokens, features = query_act.shape
    head_count = features // HD
    query_blocks = tokens // BLOCK
    reach_dev = (WIN + query_blocks - 1) // query_blocks
    total_blocks = query_blocks * cycle_size
    window_blocks = (2 * reach_dev + 1) * query_blocks
    scale = 1.0 / math.sqrt(HD)
    attn_grad = lax.dot_general(
        lax.all_gather(out_grad, "sp", axis=0, tiled=True),
        out_weight,
        CONTRACT,
        preferred_element_type=jnp.float32,
    ).astype(jnp.bfloat16)
    key_value = jnp.stack((key_act, value_act))
    gathered = jnp.concatenate(
        [
            key_value if offset == 0 else passed_along(key_value, "blk", -offset)
            for offset in range(-reach_dev, reach_dev + 1)
        ],
        axis=1,
    ).reshape(2, window_blocks, BLOCK, features)
    anchor = (my_index - reach_dev) * query_blocks
    own_lists = lax.dynamic_slice_in_dim(neighbours, my_index * query_blocks, query_blocks, 0)
    own_counts = lax.dynamic_slice_in_dim(block_counts, my_index * query_blocks, query_blocks, 0)
    window_index = ((own_lists - anchor) % total_blocks).reshape(-1)
    picked = jnp.concatenate(
        [
            lax.dynamic_slice_in_dim(gathered, window_index[n], 1, 1)
            for n in range(query_blocks * NBR)
        ],
        axis=1,
    ).reshape(2, query_blocks, NBR, BLOCK, head_count, HD)
    query_heads = query_act.reshape(query_blocks, BLOCK, head_count, HD)
    grad_heads = attn_grad.reshape(query_blocks, BLOCK, head_count, HD)
    einsum = functools.partial(jnp.einsum, preferred_element_type=jnp.float32)
    scores = scale * einsum("bihd,bsjhd->bhisj", query_heads, picked[0])
    live_slots = jnp.arange(NBR)[None, :] < own_counts[:, None]
    scores = jnp.where(live_slots[:, None, None, :, None], scores, -jnp.inf)
    row_peak = jnp.max(scores, axis=(3, 4), keepdims=True)
    log_total = row_peak + jnp.log(jnp.sum(jnp.exp(scores - row_peak), axis=(3, 4), keepdims=True))
    soft_probs = jnp.exp(scores - log_total)
    probs_half = soft_probs.astype(jnp.bfloat16)
    outputs = einsum("bhisj,bsjhd->bihd", probs_half, picked[1])
    row_delta = jnp.transpose(jnp.sum(grad_heads.astype(jnp.float32) * outputs, axis=3), (0, 2, 1))
    prob_grad = einsum("bihd,bsjhd->bhisj", grad_heads, picked[1])
    dscore_half = (soft_probs * (prob_grad - row_delta[:, :, :, None, None])).astype(jnp.bfloat16)
    query_grad = scale * einsum("bhisj,bsjhd->bihd", dscore_half, picked[0])
    query_grad = query_grad.astype(jnp.bfloat16).reshape(tokens, features)
    key_slots = scale * einsum("bhisj,bihd->bsjhd", dscore_half, query_heads)
    value_slots = einsum("bhisj,bihd->bsjhd", probs_half, grad_heads)
    slot_grads = jnp.stack((key_slots, value_slots)).reshape(
        2, query_blocks * NBR, BLOCK * features
    )
    selector = (jnp.arange(window_blocks)[:, None] == window_index.reshape(1, -1)).astype(
        jnp.float32
    )
    window_grads = jnp.einsum("wn,gnc->gwc", selector, slot_grads, precision=lax.Precision.HIGHEST)
    summed = 0.0
    for offset in range(-reach_dev, reach_dev + 1):
        first = (offset + reach_dev) * query_blocks
        portion = window_grads[:, first : first + query_blocks]
        summed = summed + (portion if offset == 0 else passed_along(portion, "blk", offset))
    own_grads = summed.reshape(2, tokens, features).astype(jnp.bfloat16)
    summed_rows = 0.0
    for grad, weight in zip((query_grad, own_grads[0], own_grads[1]), weights, strict=True):
        summed_rows = summed_rows + lax.dot_general(
            grad, weight, CONTRACT, preferred_element_type=jnp.float32
        )
    input_grad = lax.psum_scatter(summed_rows, "sp", scatter_dimension=0, tiled=True)
    return input_grad.astype(jnp.bfloat16)


def body(
    out_grad,
    query_act,
    key_act,
    value_act,
    out_weight,
    query_weight,
    key_weight,
    value_weight,
    neighbours,
    block_counts,
):
    heads = query_act.shape[1] // HD
    one_head = lax.axis_size("sp") == 1 and lax.axis_size("blk") == heads * CORES
    return (head_per_chip if one_head else by_window)(
        out_grad,
        query_act,
        key_act,
        value_act,
        out_weight,
        (query_weight, key_weight, value_weight),
        neighbours,
        block_counts,
    )


def solution(mesh):
    return jax.shard_map(
        body,
        mesh=mesh,
        in_specs=(
            P(("groups", "blk", "sp"), None),
            P(("groups", "blk"), "sp"),
            P(("groups", "blk"), "sp"),
            P(("groups", "blk"), "sp"),
            P("sp", None),
            P(None, "sp"),
            P(None, "sp"),
            P(None, "sp"),
            P("groups", None),
            P("groups"),
        ),
        out_specs=P(("groups", "blk", "sp"), None),
        check_vma=False,
    )
```

```python
import functools
import math

import jax
import jax.numpy as jnp
from jax import lax
from jax.experimental import pallas as pl
from jax.experimental.pallas import tpu as pltpu
from jax.sharding import PartitionSpec as P

HD = 128
BLOCK = 128
NBR = 8
WIN = 8
CORES = 2
WIDTHS = (2, 4, 6, 8)
GROUP = 4
AHEAD = (0, 4)
CONTRACT = (((1,), (1,)), ((), ()))
ANY = pl.BlockSpec(memory_space=pl.ANY)
VMEM = pl.BlockSpec(memory_space=pltpu.VMEM)
SMEM = pl.BlockSpec(memory_space=pltpu.SMEM)
LIMIT = pltpu.CompilerParams(vmem_limit_bytes=22 << 20)


def passed_along(shard, axis, by):
    size = lax.axis_size(axis)
    return lax.ppermute(shard, axis, [(i, (i + by) % size) for i in range(size)])


def rotated(chip, step, chips):
    return lax.rem(chip + step, chips)


def columns(head):
    return pl.ds(pl.multiple_of(head * HD, HD), HD)


def rows_of(block, size):
    return pl.ds(pl.multiple_of(block * size, size), size)


def pack_kernel(chips, chip_ref, *refs):
    sources, outs, sem = refs[:2], refs[2:-1], refs[-1]
    copies = [
        pltpu.make_async_copy(
            source.at[:, columns(rotated(chip_ref[0], step, chips))],
            outs[step].at[:, place * HD : (place + 1) * HD],
            sem.at[step * 2 + place],
        )
        for step in range(chips)
        for place, source in enumerate(sources)
    ]
    for copy in copies:
        copy.start()
    for copy in copies:
        copy.wait()


def grad_kernel(chips, chip_ref, grad_ref, weight_ref, query_ref, *outs):
    for step in range(chips):
        head = rotated(chip_ref[0], step, chips)
        outs[step][:, :HD] = query_ref[:, columns(head)]
        outs[step][:, HD:] = lax.dot_general(
            grad_ref[...],
            weight_ref[rows_of(head, HD), :],
            CONTRACT,
            preferred_element_type=jnp.float32,
        ).astype(jnp.bfloat16)


def assemble_kernel(chips, tokens, chip_ref, *refs):
    pieces, out_ref = refs[:chips], refs[chips]
    for step in range(chips):
        source = rotated(chip_ref[0], chips - step, chips)
        out_ref[rows_of(source, tokens), :] = pieces[step][...]


def turn_kernel(blocks, own_ref, other_ref, pair_ref, turned_ref, *cleared):
    for buf in cleared:
        buf[...] = jnp.zeros_like(buf)
    for side, source in enumerate((own_ref, other_ref)):
        pair_ref[side * blocks * BLOCK : (side + 1) * blocks * BLOCK] = source[...]
        for block in range(blocks):
            turned_ref[side * blocks + block] = jnp.transpose(
                source[block * BLOCK : (block + 1) * BLOCK, :HD]
            )


def attention_kernel(chips, tokens, scale, chip_ref, table_ref, count_ref, order_ref, *refs):
    pair_ref, turned_ref, pieces = refs[0], refs[1], refs[5 : 5 + chips]
    total, ask_buf, give_buf, sent_out, *dq_outs, dq_ref = refs[5 + chips :]
    blocks = chips * tokens // BLOCK
    half = blocks * BLOCK
    per_device = tokens // BLOCK
    for step in range(chips):
        source = rotated(chip_ref[0], chips - step, chips)
        for place in range(per_device):
            piece = pieces[step][place * BLOCK : (place + 1) * BLOCK, :]
            query, grad = piece[:, :HD], piece[:, HD:]
            block = source * per_device + place
            ask_buf[block, :HD, :BLOCK] = jnp.transpose(query)
            ask_buf[block, HD:, BLOCK:] = jnp.transpose(grad)
            give_buf[block, :BLOCK, :HD] = grad
            give_buf[block, BLOCK:, HD:] = query

    def attend(block, width):
        count = count_ref[block]
        index = [table_ref[block * NBR + slot] for slot in range(width)]
        slots = [rows_of(which, BLOCK) for which in index]
        pairs = jnp.concatenate([pair_ref[slot, :] for slot in slots], axis=0)
        both = jnp.dot(pairs, ask_buf[block], preferred_element_type=jnp.float32)
        scores, prob_grad = both[:, :BLOCK], both[:, BLOCK:]
        scores = jnp.concatenate(
            [
                jnp.where(slot < count, scores[slot * BLOCK : (slot + 1) * BLOCK], -jnp.inf)
                for slot in range(width)
            ],
            axis=0,
        )
        peak = jnp.max(scores, axis=0, keepdims=True)
        weights = jnp.exp2((scores - peak) * (scale * math.log2(math.e)))
        probs = weights * (1.0 / jnp.sum(weights, axis=0, keepdims=True))
        half_probs = probs.astype(jnp.bfloat16)
        delta = jnp.sum(half_probs.astype(jnp.float32) * prob_grad, axis=0, keepdims=True)
        dscore = (probs * (prob_grad - delta)).astype(jnp.bfloat16)
        turned = jnp.concatenate([turned_ref[which] for which in index], axis=1)
        dq = jnp.dot(turned, dscore, preferred_element_type=jnp.float32)
        given = jnp.dot(
            jnp.concatenate([half_probs, dscore], axis=1),
            give_buf[block],
            preferred_element_type=jnp.float32,
        )
        dq_ref[rows_of(block, BLOCK), :] = jnp.transpose(dq * scale).astype(jnp.bfloat16)
        return slots, given

    def one_group(group, carry):
        members = [order_ref[group * GROUP + member] for member in range(GROUP)]
        most = count_ref[members[0]]

        def work(width):
            for slots, given in [attend(member, width) for member in members]:
                for place, slot in enumerate(slots):
                    total[slot, :] += given[place * BLOCK : (place + 1) * BLOCK]

        below = 0
        for width in WIDTHS:
            pl.when((most > below) & (most <= width))(functools.partial(work, width))
            below = width
        return carry

    lax.fori_loop(0, blocks // GROUP, one_group, 0)
    sent_out[...] = total[half:].astype(jnp.bfloat16)
    for step in range(chips):
        rows = rows_of(rotated(chip_ref[0], chips - step, chips), tokens)
        dq_outs[step][...] = dq_ref[rows, :]


def combine_kernel(chips, tokens, scale, chip_ref, own_ref, other_ref, *refs):
    dqs, outs = refs[:chips], refs[chips:]
    for step in range(chips):
        rows = rows_of(rotated(chip_ref[0], chips - step, chips), tokens)
        summed = own_ref[rows, :] + other_ref[rows, :].astype(jnp.float32)
        outs[step][:, :HD] = dqs[step][...]
        outs[step][:, HD : 2 * HD] = (summed[:, HD:] * scale).astype(jnp.bfloat16)
        outs[step][:, 2 * HD :] = summed[:, :HD].astype(jnp.bfloat16)


def project_kernel(chips, steps, chip_ref, *refs):
    pieces, weights = refs[: len(steps)], refs[len(steps) : len(steps) + 3]
    before, (out_ref, rows_buf, weight_buf) = refs[len(steps) + 3 : -3], refs[-3:]
    total = before[0][...] if before else None
    for place in range(3):
        for at, step in enumerate(steps):
            head = rotated(chip_ref[0], step, chips)
            rows_buf[place, :, at * HD : (at + 1) * HD] = pieces[at][
                :, place * HD : (place + 1) * HD
            ]
            weight_buf[place, :, at * HD : (at + 1) * HD] = weights[place][:, columns(head)]
        part = lax.dot_general(
            rows_buf[place], weight_buf[place], CONTRACT, preferred_element_type=jnp.float32
        )
        total = part if total is None else total + part
    out_ref[...] = total.astype(out_ref.dtype)


def head_per_chip(
    out_grad, query_act, key_act, value_act, out_weight, weights, neighbours, block_counts
):
    my_index = lax.axis_index("blk")
    chips = lax.axis_size("blk") // CORES
    tokens, features = query_act.shape
    scale = 1.0 / math.sqrt(HD)
    chip = (my_index // CORES).astype(jnp.int32).reshape(1)
    core = my_index % CORES
    per_device = tokens // BLOCK
    blocks = chips * per_device
    half = chips * tokens
    bf16 = functools.partial(jax.ShapeDtypeStruct, dtype=jnp.bfloat16)
    f32 = functools.partial(jax.ShapeDtypeStruct, dtype=jnp.float32)
    buf16 = functools.partial(pltpu.VMEM, dtype=jnp.bfloat16)

    def call(kernel, outs, scratch, scalars, *arrays, spec=VMEM, aliases=()):
        return pl.pallas_call(
            kernel,
            out_shape=outs,
            in_specs=[SMEM] * len(scalars) + [spec] * len(arrays),
            out_specs=jax.tree.map(lambda _: VMEM, outs),
            scratch_shapes=scratch,
            input_output_aliases={len(scalars) + at: to for at, to in aliases},
            compiler_params=LIMIT,
        )(*scalars, *arrays)

    def by_chips(shard, step):
        pairs = [
            (CORES * c + k, CORES * ((c + step) % chips) + k)
            for c in range(chips)
            for k in range(CORES)
        ]
        return lax.ppermute(shard, "blk", pairs)

    def out_to(shards):
        return [shards[0]] + [by_chips(shards[step], step) for step in range(1, chips)]

    def across_cores(shard):
        return lax.ppermute(shard, "blk", [(i, i ^ 1) for i in range(chips * CORES)])

    own = neighbours.reshape(chips, CORES, per_device, NBR)
    own = lax.dynamic_index_in_dim(own, core, 1, keepdims=False)
    counts = block_counts.reshape(chips, CORES, per_device)
    counts = lax.dynamic_index_in_dim(counts, core, 1, keepdims=False).reshape(-1)
    holder = own // per_device
    table = (
        jnp.where(holder % CORES == core, 0, blocks)
        + (holder // CORES) * per_device
        + own % per_device
    ).reshape(-1)
    ids = jnp.arange(blocks, dtype=jnp.int32)
    rank_key = counts * blocks + ids
    rank = jnp.sum((rank_key[None, :] > rank_key[:, None]).astype(jnp.int32), axis=1)
    order = jnp.sum(jnp.where(rank[:, None] == ids[None, :], ids[:, None], 0), axis=0)

    args = functools.partial
    piece = [bf16((tokens, 2 * HD))] * chips
    pairs = call(
        args(pack_kernel, chips), piece, [pltpu.SemaphoreType.DMA((2 * chips,))],
        (chip,), *(pltpu.with_memory_space_constraint(x, pltpu.HBM) for x in (key_act, value_act)), spec=ANY,
    )
    pairs, out_grad = lax.optimization_barrier((pairs, out_grad))
    pairs = out_to(pairs)
    asks = call(args(grad_kernel, chips), piece, [], (chip,), out_grad, out_weight, query_act)
    asks = out_to(asks)
    pairs, _ = lax.optimization_barrier((pairs, [asks[step] for step in AHEAD]))
    own_pairs = call(
        args(assemble_kernel, chips, tokens), bf16((half, 2 * HD)), [], (chip,), *pairs
    )
    other_pairs = across_cores(own_pairs)
    cleared = [f32((2 * half, 2 * HD))] + [bf16((blocks, 2 * HD, 2 * BLOCK))] * 2
    both_pairs, turned, *cleared = call(
        args(turn_kernel, blocks),
        [bf16((2 * half, 2 * HD)), bf16((2 * blocks, HD, BLOCK))] + cleared, [],
        (), own_pairs, other_pairs,
    )
    sums, _, _, sent_part, *dqs = call(
        args(attention_kernel, chips, tokens, scale),
        [*(f32(c.shape) if c.dtype == jnp.float32 else bf16(c.shape) for c in cleared)]
        + [bf16((half, 2 * HD))] + [bf16((tokens, HD))] * chips,
        [buf16((half, HD))],
        (chip, table, counts, order), both_pairs, turned, *cleared, *asks,
        aliases=[(2, 0), (3, 1), (4, 2)],
    )
    came_part = across_cores(sent_part)
    back = call(
        args(combine_kernel, chips, tokens, scale), [bf16((tokens, 3 * HD))] * chips, [],
        (chip,), sums, came_part, *dqs,
    )
    back = [back[0]] + [by_chips(back[step], chips - step) for step in range(1, chips)]
    near = [min(step, chips - step) * 4 <= chips for step in range(chips)]
    early = [step for step in range(chips) if near[step]]
    late = [step for step in range(chips) if not near[step]]

    def project(steps, outs, *before):
        return call(
            args(project_kernel, chips, steps), outs,
            [buf16((3, tokens, len(steps) * HD)), buf16((3, features, len(steps) * HD))],
            (chip,), *(back[step] for step in steps), *weights, *before,
        )

    return project(late, bf16((tokens, features)), project(early, f32((tokens, features))))


def by_window(
    out_grad, query_act, key_act, value_act, out_weight, weights, neighbours, block_counts
):
    cycle_size = lax.axis_size("blk")
    my_index = lax.axis_index("blk")
    tokens, features = query_act.shape
    head_count = features // HD
    query_blocks = tokens // BLOCK
    reach_dev = (WIN + query_blocks - 1) // query_blocks
    total_blocks = query_blocks * cycle_size
    window_blocks = (2 * reach_dev + 1) * query_blocks
    scale = 1.0 / math.sqrt(HD)
    attn_grad = lax.dot_general(
        lax.all_gather(out_grad, "sp", axis=0, tiled=True),
        out_weight,
        CONTRACT,
        preferred_element_type=jnp.float32,
    ).astype(jnp.bfloat16)
    key_value = jnp.stack((key_act, value_act))
    gathered = jnp.concatenate(
        [
            key_value if offset == 0 else passed_along(key_value, "blk", -offset)
            for offset in range(-reach_dev, reach_dev + 1)
        ],
        axis=1,
    ).reshape(2, window_blocks, BLOCK, features)
    anchor = (my_index - reach_dev) * query_blocks
    own_lists = lax.dynamic_slice_in_dim(neighbours, my_index * query_blocks, query_blocks, 0)
    own_counts = lax.dynamic_slice_in_dim(block_counts, my_index * query_blocks, query_blocks, 0)
    window_index = ((own_lists - anchor) % total_blocks).reshape(-1)
    picked = jnp.concatenate(
        [
            lax.dynamic_slice_in_dim(gathered, window_index[n], 1, 1)
            for n in range(query_blocks * NBR)
        ],
        axis=1,
    ).reshape(2, query_blocks, NBR, BLOCK, head_count, HD)
    query_heads = query_act.reshape(query_blocks, BLOCK, head_count, HD)
    grad_heads = attn_grad.reshape(query_blocks, BLOCK, head_count, HD)
    einsum = functools.partial(jnp.einsum, preferred_element_type=jnp.float32)
    scores = scale * einsum("bihd,bsjhd->bhisj", query_heads, picked[0])
    live_slots = jnp.arange(NBR)[None, :] < own_counts[:, None]
    scores = jnp.where(live_slots[:, None, None, :, None], scores, -jnp.inf)
    row_peak = jnp.max(scores, axis=(3, 4), keepdims=True)
    log_total = row_peak + jnp.log(jnp.sum(jnp.exp(scores - row_peak), axis=(3, 4), keepdims=True))
    soft_probs = jnp.exp(scores - log_total)
    probs_half = soft_probs.astype(jnp.bfloat16)
    outputs = einsum("bhisj,bsjhd->bihd", probs_half, picked[1])
    row_delta = jnp.transpose(jnp.sum(grad_heads.astype(jnp.float32) * outputs, axis=3), (0, 2, 1))
    prob_grad = einsum("bihd,bsjhd->bhisj", grad_heads, picked[1])
    dscore_half = (soft_probs * (prob_grad - row_delta[:, :, :, None, None])).astype(jnp.bfloat16)
    query_grad = scale * einsum("bhisj,bsjhd->bihd", dscore_half, picked[0])
    query_grad = query_grad.astype(jnp.bfloat16).reshape(tokens, features)
    key_slots = scale * einsum("bhisj,bihd->bsjhd", dscore_half, query_heads)
    value_slots = einsum("bhisj,bihd->bsjhd", probs_half, grad_heads)
    slot_grads = jnp.stack((key_slots, value_slots)).reshape(
        2, query_blocks * NBR, BLOCK * features
    )
    selector = (jnp.arange(window_blocks)[:, None] == window_index.reshape(1, -1)).astype(
        jnp.float32
    )
    window_grads = jnp.einsum("wn,gnc->gwc", selector, slot_grads, precision=lax.Precision.HIGHEST)
    summed = 0.0
    for offset in range(-reach_dev, reach_dev + 1):
        first = (offset + reach_dev) * query_blocks
        portion = window_grads[:, first : first + query_blocks]
        summed = summed + (portion if offset == 0 else passed_along(portion, "blk", offset))
    own_grads = summed.reshape(2, tokens, features).astype(jnp.bfloat16)
    summed_rows = 0.0
    for grad, weight in zip((query_grad, own_grads[0], own_grads[1]), weights, strict=True):
        summed_rows = summed_rows + lax.dot_general(
            grad, weight, CONTRACT, preferred_element_type=jnp.float32
        )
    input_grad = lax.psum_scatter(summed_rows, "sp", scatter_dimension=0, tiled=True)
    return input_grad.astype(jnp.bfloat16)


def body(
    out_grad,
    query_act,
    key_act,
    value_act,
    out_weight,
    query_weight,
    key_weight,
    value_weight,
    neighbours,
    block_counts,
):
    heads = query_act.shape[1] // HD
    one_head = lax.axis_size("sp") == 1 and lax.axis_size("blk") == heads * CORES
    return (head_per_chip if one_head else by_window)(
        out_grad,
        query_act,
        key_act,
        value_act,
        out_weight,
        (query_weight, key_weight, value_weight),
        neighbours,
        block_counts,
    )


def solution(mesh):
    return jax.shard_map(
        body,
        mesh=mesh,
        in_specs=(
            P(("groups", "blk", "sp"), None),
            P(("groups", "blk"), "sp"),
            P(("groups", "blk"), "sp"),
            P(("groups", "blk"), "sp"),
            P("sp", None),
            P(None, "sp"),
            P(None, "sp"),
            P(None, "sp"),
            P("groups", None),
            P("groups"),
        ),
        out_specs=P(("groups", "blk", "sp"), None),
        check_vma=False,
    )
```

```python
import functools
import math

import jax
import jax.numpy as jnp
from jax import lax
from jax.experimental import pallas as pl
from jax.experimental.pallas import tpu as pltpu
from jax.sharding import PartitionSpec as P

HD = 128
BLOCK = 128
NBR = 8
WIN = 8
CORES = 2
WIDTHS = (2, 4, 6, 8)
GROUP = 4
AHEAD = (0, 4, 2)
CONTRACT = (((1,), (1,)), ((), ()))
ANY = pl.BlockSpec(memory_space=pl.ANY)
VMEM = pl.BlockSpec(memory_space=pltpu.VMEM)
SMEM = pl.BlockSpec(memory_space=pltpu.SMEM)
LIMIT = pltpu.CompilerParams(vmem_limit_bytes=22 << 20)


def passed_along(shard, axis, by):
    size = lax.axis_size(axis)
    return lax.ppermute(shard, axis, [(i, (i + by) % size) for i in range(size)])


def rotated(chip, step, chips):
    return lax.rem(chip + step, chips)


def columns(head):
    return pl.ds(pl.multiple_of(head * HD, HD), HD)


def rows_of(block, size):
    return pl.ds(pl.multiple_of(block * size, size), size)


def pack_kernel(chips, chip_ref, *refs):
    sources, outs, sem = refs[:2], refs[2:-1], refs[-1]
    copies = [
        pltpu.make_async_copy(
            source.at[:, columns(rotated(chip_ref[0], step, chips))],
            outs[step].at[:, place * HD : (place + 1) * HD],
            sem.at[step * 2 + place],
        )
        for step in range(chips)
        for place, source in enumerate(sources)
    ]
    for copy in copies:
        copy.start()
    for copy in copies:
        copy.wait()


def grad_kernel(chips, chip_ref, grad_ref, weight_ref, query_ref, *outs):
    for step in range(chips):
        head = rotated(chip_ref[0], step, chips)
        outs[step][:, :HD] = query_ref[:, columns(head)]
        outs[step][:, HD:] = lax.dot_general(
            grad_ref[...],
            weight_ref[rows_of(head, HD), :],
            CONTRACT,
            preferred_element_type=jnp.float32,
        ).astype(jnp.bfloat16)


def assemble_kernel(chips, tokens, chip_ref, *refs):
    pieces, out_ref = refs[:chips], refs[chips]
    for step in range(chips):
        source = rotated(chip_ref[0], chips - step, chips)
        out_ref[rows_of(source, tokens), :] = pieces[step][...]


def turn_kernel(blocks, own_ref, other_ref, pair_ref, turned_ref, *cleared):
    for buf in cleared:
        buf[...] = jnp.zeros_like(buf)
    for side, source in enumerate((own_ref, other_ref)):
        pair_ref[side * blocks * BLOCK : (side + 1) * blocks * BLOCK] = source[...]
        for block in range(blocks):
            turned_ref[side * blocks + block] = jnp.transpose(
                source[block * BLOCK : (block + 1) * BLOCK, :HD]
            )


def attention_kernel(chips, tokens, scale, chip_ref, table_ref, count_ref, order_ref, *refs):
    pair_ref, turned_ref, pieces = refs[0], refs[1], refs[5 : 5 + chips]
    total, ask_buf, give_buf, sent_out, *dq_outs, dq_ref = refs[5 + chips :]
    blocks = chips * tokens // BLOCK
    half = blocks * BLOCK
    per_device = tokens // BLOCK
    for step in range(chips):
        source = rotated(chip_ref[0], chips - step, chips)
        for place in range(per_device):
            piece = pieces[step][place * BLOCK : (place + 1) * BLOCK, :]
            query, grad = piece[:, :HD], piece[:, HD:]
            block = source * per_device + place
            ask_buf[block, :HD, :BLOCK] = jnp.transpose(query)
            ask_buf[block, HD:, BLOCK:] = jnp.transpose(grad)
            give_buf[block, :BLOCK, :HD] = grad
            give_buf[block, BLOCK:, HD:] = query

    def attend(block, width):
        count = count_ref[block]
        index = [table_ref[block * NBR + slot] for slot in range(width)]
        slots = [rows_of(which, BLOCK) for which in index]
        pairs = jnp.concatenate([pair_ref[slot, :] for slot in slots], axis=0)
        both = jnp.dot(pairs, ask_buf[block], preferred_element_type=jnp.float32)
        scores, prob_grad = both[:, :BLOCK], both[:, BLOCK:]
        scores = jnp.concatenate(
            [
                jnp.where(slot < count, scores[slot * BLOCK : (slot + 1) * BLOCK], -jnp.inf)
                for slot in range(width)
            ],
            axis=0,
        )
        peak = jnp.max(scores, axis=0, keepdims=True)
        weights = jnp.exp2((scores - peak) * (scale * math.log2(math.e)))
        probs = weights * (1.0 / jnp.sum(weights, axis=0, keepdims=True))
        half_probs = probs.astype(jnp.bfloat16)
        delta = jnp.sum(half_probs.astype(jnp.float32) * prob_grad, axis=0, keepdims=True)
        dscore = (probs * (prob_grad - delta)).astype(jnp.bfloat16)
        turned = jnp.concatenate([turned_ref[which] for which in index], axis=1)
        dq = jnp.dot(turned, dscore, preferred_element_type=jnp.float32)
        given = jnp.dot(
            jnp.concatenate([half_probs, dscore], axis=1),
            give_buf[block],
            preferred_element_type=jnp.float32,
        )
        dq_ref[rows_of(block, BLOCK), :] = jnp.transpose(dq * scale).astype(jnp.bfloat16)
        return slots, given

    def one_group(group, carry):
        members = [order_ref[group * GROUP + member] for member in range(GROUP)]
        most = count_ref[members[0]]

        def work(width):
            for slots, given in [attend(member, width) for member in members]:
                for place, slot in enumerate(slots):
                    total[slot, :] += given[place * BLOCK : (place + 1) * BLOCK]

        below = 0
        for width in WIDTHS:
            pl.when((most > below) & (most <= width))(functools.partial(work, width))
            below = width
        return carry

    lax.fori_loop(0, blocks // GROUP, one_group, 0)
    sent_out[...] = total[half:].astype(jnp.bfloat16)
    for step in range(chips):
        rows = rows_of(rotated(chip_ref[0], chips - step, chips), tokens)
        dq_outs[step][...] = dq_ref[rows, :]


def combine_kernel(chips, tokens, scale, chip_ref, own_ref, other_ref, *refs):
    dqs, outs = refs[:chips], refs[chips:]
    for step in range(chips):
        rows = rows_of(rotated(chip_ref[0], chips - step, chips), tokens)
        summed = own_ref[rows, :] + other_ref[rows, :].astype(jnp.float32)
        outs[step][:, :HD] = dqs[step][...]
        outs[step][:, HD : 2 * HD] = (summed[:, HD:] * scale).astype(jnp.bfloat16)
        outs[step][:, 2 * HD :] = summed[:, :HD].astype(jnp.bfloat16)


def project_kernel(chips, steps, chip_ref, *refs):
    pieces, weights = refs[: len(steps)], refs[len(steps) : len(steps) + 3]
    before, (out_ref, rows_buf, weight_buf) = refs[len(steps) + 3 : -3], refs[-3:]
    total = before[0][...] if before else None
    for place in range(3):
        for at, step in enumerate(steps):
            head = rotated(chip_ref[0], step, chips)
            rows_buf[place, :, at * HD : (at + 1) * HD] = pieces[at][
                :, place * HD : (place + 1) * HD
            ]
            weight_buf[place, :, at * HD : (at + 1) * HD] = weights[place][:, columns(head)]
        part = lax.dot_general(
            rows_buf[place], weight_buf[place], CONTRACT, preferred_element_type=jnp.float32
        )
        total = part if total is None else total + part
    out_ref[...] = total.astype(out_ref.dtype)


def head_per_chip(
    out_grad, query_act, key_act, value_act, out_weight, weights, neighbours, block_counts
):
    my_index = lax.axis_index("blk")
    chips = lax.axis_size("blk") // CORES
    tokens, features = query_act.shape
    scale = 1.0 / math.sqrt(HD)
    chip = (my_index // CORES).astype(jnp.int32).reshape(1)
    core = my_index % CORES
    per_device = tokens // BLOCK
    blocks = chips * per_device
    half = chips * tokens
    bf16 = functools.partial(jax.ShapeDtypeStruct, dtype=jnp.bfloat16)
    f32 = functools.partial(jax.ShapeDtypeStruct, dtype=jnp.float32)
    buf16 = functools.partial(pltpu.VMEM, dtype=jnp.bfloat16)

    def call(kernel, outs, scratch, scalars, *arrays, spec=VMEM, aliases=()):
        return pl.pallas_call(
            kernel,
            out_shape=outs,
            in_specs=[SMEM] * len(scalars) + [spec] * len(arrays),
            out_specs=jax.tree.map(lambda _: VMEM, outs),
            scratch_shapes=scratch,
            input_output_aliases={len(scalars) + at: to for at, to in aliases},
            compiler_params=LIMIT,
        )(*scalars, *arrays)

    def by_chips(shard, step):
        pairs = [
            (CORES * c + k, CORES * ((c + step) % chips) + k)
            for c in range(chips)
            for k in range(CORES)
        ]
        return lax.ppermute(shard, "blk", pairs)

    def out_to(shards):
        return [shards[0]] + [by_chips(shards[step], step) for step in range(1, chips)]

    def across_cores(shard):
        return lax.ppermute(shard, "blk", [(i, i ^ 1) for i in range(chips * CORES)])

    own = neighbours.reshape(chips, CORES, per_device, NBR)
    own = lax.dynamic_index_in_dim(own, core, 1, keepdims=False)
    counts = block_counts.reshape(chips, CORES, per_device)
    counts = lax.dynamic_index_in_dim(counts, core, 1, keepdims=False).reshape(-1)
    holder = own // per_device
    table = (
        jnp.where(holder % CORES == core, 0, blocks)
        + (holder // CORES) * per_device
        + own % per_device
    ).reshape(-1)
    ids = jnp.arange(blocks, dtype=jnp.int32)
    rank_key = counts * blocks + ids
    rank = jnp.sum((rank_key[None, :] > rank_key[:, None]).astype(jnp.int32), axis=1)
    order = jnp.sum(jnp.where(rank[:, None] == ids[None, :], ids[:, None], 0), axis=0)

    args = functools.partial
    piece = [bf16((tokens, 2 * HD))] * chips
    pairs = call(
        args(pack_kernel, chips), piece, [pltpu.SemaphoreType.DMA((2 * chips,))],
        (chip,), *(pltpu.with_memory_space_constraint(x, pltpu.HBM) for x in (key_act, value_act)), spec=ANY,
    )
    pairs, out_grad = lax.optimization_barrier((pairs, out_grad))
    pairs = out_to(pairs)
    asks = call(args(grad_kernel, chips), piece, [], (chip,), out_grad, out_weight, query_act)
    asks = out_to(asks)
    pairs, _ = lax.optimization_barrier((pairs, [asks[step] for step in AHEAD]))
    own_pairs = call(
        args(assemble_kernel, chips, tokens), bf16((half, 2 * HD)), [], (chip,), *pairs
    )
    other_pairs = across_cores(own_pairs)
    cleared = [f32((2 * half, 2 * HD))] + [bf16((blocks, 2 * HD, 2 * BLOCK))] * 2
    both_pairs, turned, *cleared = call(
        args(turn_kernel, blocks),
        [bf16((2 * half, 2 * HD)), bf16((2 * blocks, HD, BLOCK))] + cleared, [],
        (), own_pairs, other_pairs,
    )
    sums, _, _, sent_part, *dqs = call(
        args(attention_kernel, chips, tokens, scale),
        [*(f32(c.shape) if c.dtype == jnp.float32 else bf16(c.shape) for c in cleared)]
        + [bf16((half, 2 * HD))] + [bf16((tokens, HD))] * chips,
        [buf16((half, HD))],
        (chip, table, counts, order), both_pairs, turned, *cleared, *asks,
        aliases=[(2, 0), (3, 1), (4, 2)],
    )
    came_part = across_cores(sent_part)
    back = call(
        args(combine_kernel, chips, tokens, scale), [bf16((tokens, 3 * HD))] * chips, [],
        (chip,), sums, came_part, *dqs,
    )
    back = [back[0]] + [by_chips(back[step], chips - step) for step in range(1, chips)]
    near = [min(step, chips - step) * 8 <= 3 * chips for step in range(chips)]
    early = [step for step in range(chips) if near[step]]
    late = [step for step in range(chips) if not near[step]]

    def project(steps, outs, *before):
        return call(
            args(project_kernel, chips, steps), outs,
            [buf16((3, tokens, len(steps) * HD)), buf16((3, features, len(steps) * HD))],
            (chip,), *(back[step] for step in steps), *weights, *before,
        )

    return project(late, bf16((tokens, features)), project(early, f32((tokens, features))))


def by_window(
    out_grad, query_act, key_act, value_act, out_weight, weights, neighbours, block_counts
):
    cycle_size = lax.axis_size("blk")
    my_index = lax.axis_index("blk")
    tokens, features = query_act.shape
    head_count = features // HD
    query_blocks = tokens // BLOCK
    reach_dev = (WIN + query_blocks - 1) // query_blocks
    total_blocks = query_blocks * cycle_size
    window_blocks = (2 * reach_dev + 1) * query_blocks
    scale = 1.0 / math.sqrt(HD)
    attn_grad = lax.dot_general(
        lax.all_gather(out_grad, "sp", axis=0, tiled=True),
        out_weight,
        CONTRACT,
        preferred_element_type=jnp.float32,
    ).astype(jnp.bfloat16)
    key_value = jnp.stack((key_act, value_act))
    gathered = jnp.concatenate(
        [
            key_value if offset == 0 else passed_along(key_value, "blk", -offset)
            for offset in range(-reach_dev, reach_dev + 1)
        ],
        axis=1,
    ).reshape(2, window_blocks, BLOCK, features)
    anchor = (my_index - reach_dev) * query_blocks
    own_lists = lax.dynamic_slice_in_dim(neighbours, my_index * query_blocks, query_blocks, 0)
    own_counts = lax.dynamic_slice_in_dim(block_counts, my_index * query_blocks, query_blocks, 0)
    window_index = ((own_lists - anchor) % total_blocks).reshape(-1)
    picked = jnp.concatenate(
        [
            lax.dynamic_slice_in_dim(gathered, window_index[n], 1, 1)
            for n in range(query_blocks * NBR)
        ],
        axis=1,
    ).reshape(2, query_blocks, NBR, BLOCK, head_count, HD)
    query_heads = query_act.reshape(query_blocks, BLOCK, head_count, HD)
    grad_heads = attn_grad.reshape(query_blocks, BLOCK, head_count, HD)
    einsum = functools.partial(jnp.einsum, preferred_element_type=jnp.float32)
    scores = scale * einsum("bihd,bsjhd->bhisj", query_heads, picked[0])
    live_slots = jnp.arange(NBR)[None, :] < own_counts[:, None]
    scores = jnp.where(live_slots[:, None, None, :, None], scores, -jnp.inf)
    row_peak = jnp.max(scores, axis=(3, 4), keepdims=True)
    log_total = row_peak + jnp.log(jnp.sum(jnp.exp(scores - row_peak), axis=(3, 4), keepdims=True))
    soft_probs = jnp.exp(scores - log_total)
    probs_half = soft_probs.astype(jnp.bfloat16)
    outputs = einsum("bhisj,bsjhd->bihd", probs_half, picked[1])
    row_delta = jnp.transpose(jnp.sum(grad_heads.astype(jnp.float32) * outputs, axis=3), (0, 2, 1))
    prob_grad = einsum("bihd,bsjhd->bhisj", grad_heads, picked[1])
    dscore_half = (soft_probs * (prob_grad - row_delta[:, :, :, None, None])).astype(jnp.bfloat16)
    query_grad = scale * einsum("bhisj,bsjhd->bihd", dscore_half, picked[0])
    query_grad = query_grad.astype(jnp.bfloat16).reshape(tokens, features)
    key_slots = scale * einsum("bhisj,bihd->bsjhd", dscore_half, query_heads)
    value_slots = einsum("bhisj,bihd->bsjhd", probs_half, grad_heads)
    slot_grads = jnp.stack((key_slots, value_slots)).reshape(
        2, query_blocks * NBR, BLOCK * features
    )
    selector = (jnp.arange(window_blocks)[:, None] == window_index.reshape(1, -1)).astype(
        jnp.float32
    )
    window_grads = jnp.einsum("wn,gnc->gwc", selector, slot_grads, precision=lax.Precision.HIGHEST)
    summed = 0.0
    for offset in range(-reach_dev, reach_dev + 1):
        first = (offset + reach_dev) * query_blocks
        portion = window_grads[:, first : first + query_blocks]
        summed = summed + (portion if offset == 0 else passed_along(portion, "blk", offset))
    own_grads = summed.reshape(2, tokens, features).astype(jnp.bfloat16)
    summed_rows = 0.0
    for grad, weight in zip((query_grad, own_grads[0], own_grads[1]), weights, strict=True):
        summed_rows = summed_rows + lax.dot_general(
            grad, weight, CONTRACT, preferred_element_type=jnp.float32
        )
    input_grad = lax.psum_scatter(summed_rows, "sp", scatter_dimension=0, tiled=True)
    return input_grad.astype(jnp.bfloat16)


def body(
    out_grad,
    query_act,
    key_act,
    value_act,
    out_weight,
    query_weight,
    key_weight,
    value_weight,
    neighbours,
    block_counts,
):
    heads = query_act.shape[1] // HD
    one_head = lax.axis_size("sp") == 1 and lax.axis_size("blk") == heads * CORES
    return (head_per_chip if one_head else by_window)(
        out_grad,
        query_act,
        key_act,
        value_act,
        out_weight,
        (query_weight, key_weight, value_weight),
        neighbours,
        block_counts,
    )


def solution(mesh):
    return jax.shard_map(
        body,
        mesh=mesh,
        in_specs=(
            P(("groups", "blk", "sp"), None),
            P(("groups", "blk"), "sp"),
            P(("groups", "blk"), "sp"),
            P(("groups", "blk"), "sp"),
            P("sp", None),
            P(None, "sp"),
            P(None, "sp"),
            P(None, "sp"),
            P("groups", None),
            P("groups"),
        ),
        out_specs=P(("groups", "blk", "sp"), None),
        check_vma=False,
    )
```

```python
import functools
import math

import jax
import jax.numpy as jnp
from jax import lax
from jax.experimental import pallas as pl
from jax.experimental.pallas import tpu as pltpu
from jax.sharding import PartitionSpec as P

HD = 128
BLOCK = 128
NBR = 8
WIN = 8
CORES = 2
WIDTHS = (2, 4, 8)
GROUP = 4
AHEAD = (0, 4, 2)
CONTRACT = (((1,), (1,)), ((), ()))
ANY = pl.BlockSpec(memory_space=pl.ANY)
VMEM = pl.BlockSpec(memory_space=pltpu.VMEM)
SMEM = pl.BlockSpec(memory_space=pltpu.SMEM)
LIMIT = pltpu.CompilerParams(vmem_limit_bytes=22 << 20)


def passed_along(shard, axis, by):
    size = lax.axis_size(axis)
    return lax.ppermute(shard, axis, [(i, (i + by) % size) for i in range(size)])


def rotated(chip, step, chips):
    return lax.rem(chip + step, chips)


def columns(head):
    return pl.ds(pl.multiple_of(head * HD, HD), HD)


def rows_of(block, size):
    return pl.ds(pl.multiple_of(block * size, size), size)


def pack_kernel(chips, chip_ref, *refs):
    sources, outs, sem = refs[:2], refs[2:-1], refs[-1]
    copies = [
        pltpu.make_async_copy(
            source.at[:, columns(rotated(chip_ref[0], step, chips))],
            outs[step].at[:, place * HD : (place + 1) * HD],
            sem.at[step * 2 + place],
        )
        for step in range(chips)
        for place, source in enumerate(sources)
    ]
    for copy in copies:
        copy.start()
    for copy in copies:
        copy.wait()


def grad_kernel(chips, chip_ref, grad_ref, weight_ref, query_ref, *outs):
    for step in range(chips):
        head = rotated(chip_ref[0], step, chips)
        outs[step][:, :HD] = query_ref[:, columns(head)]
        outs[step][:, HD:] = lax.dot_general(
            grad_ref[...],
            weight_ref[rows_of(head, HD), :],
            CONTRACT,
            preferred_element_type=jnp.float32,
        ).astype(jnp.bfloat16)


def assemble_kernel(chips, tokens, chip_ref, *refs):
    pieces, out_ref = refs[:chips], refs[chips]
    for step in range(chips):
        source = rotated(chip_ref[0], chips - step, chips)
        out_ref[rows_of(source, tokens), :] = pieces[step][...]


def turn_kernel(blocks, own_ref, other_ref, pair_ref, turned_ref, *cleared):
    for buf in cleared:
        buf[...] = jnp.zeros_like(buf)
    for side, source in enumerate((own_ref, other_ref)):
        pair_ref[side * blocks * BLOCK : (side + 1) * blocks * BLOCK] = source[...]
        for block in range(blocks):
            turned_ref[side * blocks + block] = jnp.transpose(
                source[block * BLOCK : (block + 1) * BLOCK, :HD]
            )


def attention_kernel(chips, tokens, scale, chip_ref, table_ref, count_ref, order_ref, *refs):
    pair_ref, turned_ref, pieces = refs[0], refs[1], refs[5 : 5 + chips]
    total, ask_buf, give_buf, sent_out, *dq_outs, dq_ref = refs[5 + chips :]
    blocks = chips * tokens // BLOCK
    half = blocks * BLOCK
    per_device = tokens // BLOCK
    for step in range(chips):
        source = rotated(chip_ref[0], chips - step, chips)
        for place in range(per_device):
            piece = pieces[step][place * BLOCK : (place + 1) * BLOCK, :]
            query, grad = piece[:, :HD], piece[:, HD:]
            block = source * per_device + place
            ask_buf[block, :HD, :BLOCK] = jnp.transpose(query)
            ask_buf[block, HD:, BLOCK:] = jnp.transpose(grad)
            give_buf[block, :BLOCK, :HD] = grad
            give_buf[block, BLOCK:, HD:] = query

    def attend(block, width):
        count = count_ref[block]
        index = [table_ref[block * NBR + slot] for slot in range(width)]
        slots = [rows_of(which, BLOCK) for which in index]
        pairs = jnp.concatenate([pair_ref[slot, :] for slot in slots], axis=0)
        both = jnp.dot(pairs, ask_buf[block], preferred_element_type=jnp.float32)
        scores, prob_grad = both[:, :BLOCK], both[:, BLOCK:]
        scores = jnp.concatenate(
            [
                jnp.where(slot < count, scores[slot * BLOCK : (slot + 1) * BLOCK], -jnp.inf)
                for slot in range(width)
            ],
            axis=0,
        )
        peak = jnp.max(scores, axis=0, keepdims=True)
        weights = jnp.exp2((scores - peak) * (scale * math.log2(math.e)))
        probs = weights * (1.0 / jnp.sum(weights, axis=0, keepdims=True))
        half_probs = probs.astype(jnp.bfloat16)
        delta = jnp.sum(half_probs.astype(jnp.float32) * prob_grad, axis=0, keepdims=True)
        dscore = (probs * (prob_grad - delta)).astype(jnp.bfloat16)
        turned = jnp.concatenate([turned_ref[which] for which in index], axis=1)
        dq = jnp.dot(turned, dscore, preferred_element_type=jnp.float32)
        given = jnp.dot(
            jnp.concatenate([half_probs, dscore], axis=1),
            give_buf[block],
            preferred_element_type=jnp.float32,
        )
        dq_ref[rows_of(block, BLOCK), :] = jnp.transpose(dq * scale).astype(jnp.bfloat16)
        return slots, given

    def one_group(group, carry):
        members = [order_ref[group * GROUP + member] for member in range(GROUP)]
        most = count_ref[members[0]]

        def work(width):
            for slots, given in [attend(member, width) for member in members]:
                for place, slot in enumerate(slots):
                    total[slot, :] += given[place * BLOCK : (place + 1) * BLOCK]

        below = 0
        for width in WIDTHS:
            pl.when((most > below) & (most <= width))(functools.partial(work, width))
            below = width
        return carry

    lax.fori_loop(0, blocks // GROUP, one_group, 0)
    sent_out[...] = total[half:].astype(jnp.bfloat16)
    for step in range(chips):
        rows = rows_of(rotated(chip_ref[0], chips - step, chips), tokens)
        dq_outs[step][...] = dq_ref[rows, :]


def combine_kernel(chips, tokens, scale, chip_ref, own_ref, other_ref, *refs):
    dqs, outs = refs[:chips], refs[chips:]
    for step in range(chips):
        rows = rows_of(rotated(chip_ref[0], chips - step, chips), tokens)
        summed = own_ref[rows, :] + other_ref[rows, :].astype(jnp.float32)
        outs[step][:, :HD] = dqs[step][...]
        outs[step][:, HD : 2 * HD] = (summed[:, HD:] * scale).astype(jnp.bfloat16)
        outs[step][:, 2 * HD :] = summed[:, :HD].astype(jnp.bfloat16)


def project_kernel(chips, steps, chip_ref, *refs):
    pieces, weights = refs[: len(steps)], refs[len(steps) : len(steps) + 3]
    before, (out_ref, rows_buf, weight_buf) = refs[len(steps) + 3 : -3], refs[-3:]
    total = before[0][...] if before else None
    for place in range(3):
        for at, step in enumerate(steps):
            head = rotated(chip_ref[0], step, chips)
            rows_buf[place, :, at * HD : (at + 1) * HD] = pieces[at][
                :, place * HD : (place + 1) * HD
            ]
            weight_buf[place, :, at * HD : (at + 1) * HD] = weights[place][:, columns(head)]
        part = lax.dot_general(
            rows_buf[place], weight_buf[place], CONTRACT, preferred_element_type=jnp.float32
        )
        total = part if total is None else total + part
    out_ref[...] = total.astype(out_ref.dtype)


def head_per_chip(
    out_grad, query_act, key_act, value_act, out_weight, weights, neighbours, block_counts
):
    my_index = lax.axis_index("blk")
    chips = lax.axis_size("blk") // CORES
    tokens, features = query_act.shape
    scale = 1.0 / math.sqrt(HD)
    chip = (my_index // CORES).astype(jnp.int32).reshape(1)
    core = my_index % CORES
    per_device = tokens // BLOCK
    blocks = chips * per_device
    half = chips * tokens
    bf16 = functools.partial(jax.ShapeDtypeStruct, dtype=jnp.bfloat16)
    f32 = functools.partial(jax.ShapeDtypeStruct, dtype=jnp.float32)
    buf16 = functools.partial(pltpu.VMEM, dtype=jnp.bfloat16)

    def call(kernel, outs, scratch, scalars, *arrays, spec=VMEM, aliases=()):
        return pl.pallas_call(
            kernel,
            out_shape=outs,
            in_specs=[SMEM] * len(scalars) + [spec] * len(arrays),
            out_specs=jax.tree.map(lambda _: VMEM, outs),
            scratch_shapes=scratch,
            input_output_aliases={len(scalars) + at: to for at, to in aliases},
            compiler_params=LIMIT,
        )(*scalars, *arrays)

    def by_chips(shard, step):
        pairs = [
            (CORES * c + k, CORES * ((c + step) % chips) + k)
            for c in range(chips)
            for k in range(CORES)
        ]
        return lax.ppermute(shard, "blk", pairs)

    def out_to(shards):
        return [shards[0]] + [by_chips(shards[step], step) for step in range(1, chips)]

    def across_cores(shard):
        return lax.ppermute(shard, "blk", [(i, i ^ 1) for i in range(chips * CORES)])

    own = neighbours.reshape(chips, CORES, per_device, NBR)
    own = lax.dynamic_index_in_dim(own, core, 1, keepdims=False)
    counts = block_counts.reshape(chips, CORES, per_device)
    counts = lax.dynamic_index_in_dim(counts, core, 1, keepdims=False).reshape(-1)
    holder = own // per_device
    table = (
        jnp.where(holder % CORES == core, 0, blocks)
        + (holder // CORES) * per_device
        + own % per_device
    ).reshape(-1)
    ids = jnp.arange(blocks, dtype=jnp.int32)
    rank_key = counts * blocks + ids
    rank = jnp.sum((rank_key[None, :] > rank_key[:, None]).astype(jnp.int32), axis=1)
    order = jnp.sum(jnp.where(rank[:, None] == ids[None, :], ids[:, None], 0), axis=0)

    args = functools.partial
    piece = [bf16((tokens, 2 * HD))] * chips
    pairs = call(
        args(pack_kernel, chips), piece, [pltpu.SemaphoreType.DMA((2 * chips,))],
        (chip,), *(pltpu.with_memory_space_constraint(x, pltpu.HBM) for x in (key_act, value_act)), spec=ANY,
    )
    pairs, out_grad = lax.optimization_barrier((pairs, out_grad))
    pairs = out_to(pairs)
    asks = call(args(grad_kernel, chips), piece, [], (chip,), out_grad, out_weight, query_act)
    asks = out_to(asks)
    pairs, _ = lax.optimization_barrier((pairs, [asks[step] for step in AHEAD]))
    own_pairs = call(
        args(assemble_kernel, chips, tokens), bf16((half, 2 * HD)), [], (chip,), *pairs
    )
    other_pairs = across_cores(own_pairs)
    cleared = [f32((2 * half, 2 * HD))] + [bf16((blocks, 2 * HD, 2 * BLOCK))] * 2
    both_pairs, turned, *cleared = call(
        args(turn_kernel, blocks),
        [bf16((2 * half, 2 * HD)), bf16((2 * blocks, HD, BLOCK))] + cleared, [],
        (), own_pairs, other_pairs,
    )
    sums, _, _, sent_part, *dqs = call(
        args(attention_kernel, chips, tokens, scale),
        [*(f32(c.shape) if c.dtype == jnp.float32 else bf16(c.shape) for c in cleared)]
        + [bf16((half, 2 * HD))] + [bf16((tokens, HD))] * chips,
        [buf16((half, HD))],
        (chip, table, counts, order), both_pairs, turned, *cleared, *asks,
        aliases=[(2, 0), (3, 1), (4, 2)],
    )
    came_part = across_cores(sent_part)
    back = call(
        args(combine_kernel, chips, tokens, scale), [bf16((tokens, 3 * HD))] * chips, [],
        (chip,), sums, came_part, *dqs,
    )
    back = [back[0]] + [by_chips(back[step], chips - step) for step in range(1, chips)]
    near = [min(step, chips - step) * 8 <= 3 * chips for step in range(chips)]
    early = [step for step in range(chips) if near[step]]
    late = [step for step in range(chips) if not near[step]]

    def project(steps, outs, *before):
        return call(
            args(project_kernel, chips, steps), outs,
            [buf16((3, tokens, len(steps) * HD)), buf16((3, features, len(steps) * HD))],
            (chip,), *(back[step] for step in steps), *weights, *before,
        )

    return project(late, bf16((tokens, features)), project(early, f32((tokens, features))))


def by_window(
    out_grad, query_act, key_act, value_act, out_weight, weights, neighbours, block_counts
):
    cycle_size = lax.axis_size("blk")
    my_index = lax.axis_index("blk")
    tokens, features = query_act.shape
    head_count = features // HD
    query_blocks = tokens // BLOCK
    reach_dev = (WIN + query_blocks - 1) // query_blocks
    total_blocks = query_blocks * cycle_size
    window_blocks = (2 * reach_dev + 1) * query_blocks
    scale = 1.0 / math.sqrt(HD)
    attn_grad = lax.dot_general(
        lax.all_gather(out_grad, "sp", axis=0, tiled=True),
        out_weight,
        CONTRACT,
        preferred_element_type=jnp.float32,
    ).astype(jnp.bfloat16)
    key_value = jnp.stack((key_act, value_act))
    gathered = jnp.concatenate(
        [
            key_value if offset == 0 else passed_along(key_value, "blk", -offset)
            for offset in range(-reach_dev, reach_dev + 1)
        ],
        axis=1,
    ).reshape(2, window_blocks, BLOCK, features)
    anchor = (my_index - reach_dev) * query_blocks
    own_lists = lax.dynamic_slice_in_dim(neighbours, my_index * query_blocks, query_blocks, 0)
    own_counts = lax.dynamic_slice_in_dim(block_counts, my_index * query_blocks, query_blocks, 0)
    window_index = ((own_lists - anchor) % total_blocks).reshape(-1)
    picked = jnp.concatenate(
        [
            lax.dynamic_slice_in_dim(gathered, window_index[n], 1, 1)
            for n in range(query_blocks * NBR)
        ],
        axis=1,
    ).reshape(2, query_blocks, NBR, BLOCK, head_count, HD)
    query_heads = query_act.reshape(query_blocks, BLOCK, head_count, HD)
    grad_heads = attn_grad.reshape(query_blocks, BLOCK, head_count, HD)
    einsum = functools.partial(jnp.einsum, preferred_element_type=jnp.float32)
    scores = scale * einsum("bihd,bsjhd->bhisj", query_heads, picked[0])
    live_slots = jnp.arange(NBR)[None, :] < own_counts[:, None]
    scores = jnp.where(live_slots[:, None, None, :, None], scores, -jnp.inf)
    row_peak = jnp.max(scores, axis=(3, 4), keepdims=True)
    log_total = row_peak + jnp.log(jnp.sum(jnp.exp(scores - row_peak), axis=(3, 4), keepdims=True))
    soft_probs = jnp.exp(scores - log_total)
    probs_half = soft_probs.astype(jnp.bfloat16)
    outputs = einsum("bhisj,bsjhd->bihd", probs_half, picked[1])
    row_delta = jnp.transpose(jnp.sum(grad_heads.astype(jnp.float32) * outputs, axis=3), (0, 2, 1))
    prob_grad = einsum("bihd,bsjhd->bhisj", grad_heads, picked[1])
    dscore_half = (soft_probs * (prob_grad - row_delta[:, :, :, None, None])).astype(jnp.bfloat16)
    query_grad = scale * einsum("bhisj,bsjhd->bihd", dscore_half, picked[0])
    query_grad = query_grad.astype(jnp.bfloat16).reshape(tokens, features)
    key_slots = scale * einsum("bhisj,bihd->bsjhd", dscore_half, query_heads)
    value_slots = einsum("bhisj,bihd->bsjhd", probs_half, grad_heads)
    slot_grads = jnp.stack((key_slots, value_slots)).reshape(
        2, query_blocks * NBR, BLOCK * features
    )
    selector = (jnp.arange(window_blocks)[:, None] == window_index.reshape(1, -1)).astype(
        jnp.float32
    )
    window_grads = jnp.einsum("wn,gnc->gwc", selector, slot_grads, precision=lax.Precision.HIGHEST)
    summed = 0.0
    for offset in range(-reach_dev, reach_dev + 1):
        first = (offset + reach_dev) * query_blocks
        portion = window_grads[:, first : first + query_blocks]
        summed = summed + (portion if offset == 0 else passed_along(portion, "blk", offset))
    own_grads = summed.reshape(2, tokens, features).astype(jnp.bfloat16)
    summed_rows = 0.0
    for grad, weight in zip((query_grad, own_grads[0], own_grads[1]), weights, strict=True):
        summed_rows = summed_rows + lax.dot_general(
            grad, weight, CONTRACT, preferred_element_type=jnp.float32
        )
    input_grad = lax.psum_scatter(summed_rows, "sp", scatter_dimension=0, tiled=True)
    return input_grad.astype(jnp.bfloat16)


def body(
    out_grad,
    query_act,
    key_act,
    value_act,
    out_weight,
    query_weight,
    key_weight,
    value_weight,
    neighbours,
    block_counts,
):
    heads = query_act.shape[1] // HD
    one_head = lax.axis_size("sp") == 1 and lax.axis_size("blk") == heads * CORES
    return (head_per_chip if one_head else by_window)(
        out_grad,
        query_act,
        key_act,
        value_act,
        out_weight,
        (query_weight, key_weight, value_weight),
        neighbours,
        block_counts,
    )


def solution(mesh):
    return jax.shard_map(
        body,
        mesh=mesh,
        in_specs=(
            P(("groups", "blk", "sp"), None),
            P(("groups", "blk"), "sp"),
            P(("groups", "blk"), "sp"),
            P(("groups", "blk"), "sp"),
            P("sp", None),
            P(None, "sp"),
            P(None, "sp"),
            P(None, "sp"),
            P("groups", None),
            P("groups"),
        ),
        out_specs=P(("groups", "blk", "sp"), None),
        check_vma=False,
    )
```
